128 devices in a mesh: row: 32 (over y, x, core), col: 4 (over z).
Axes of the slice: x: 4, y: 4, z: 4, core: 2. Of those that a mesh axis runs over, the one named last changes fastest.
Arguments:
- coeffs: bfloat16 [8192, 2048], P('row', 'col'), may hold values from -1.5 to 1.5
- basis_values: bfloat16 [128, 512, 512], P(('row', 'col')), may hold values from -1 to 1
- point_weights: float32 [128, 512], P(('row', 'col')), may hold values from 0.05 to 1
- point_counts: int32 [128], P(('row', 'col')), may hold values from 1 to 512, as said below
- func_lists: int32 [128, 512], P(('row', 'col')), may hold values from 0 to 8191, as said below
Outputs:
- density: bfloat16 [8192, 8192], P('col', 'row')
- potential: float32 [8192, 8192], P('col', 'row')
The draws below stay inside these ranges and needn't reach their ends.
Inputs may be any that keep to these rules, and one draw needn't show every extreme that they name: `func_lists`: A batch held by device index d of row+col has its functions in the three row-axis blocks (d // 4 - 1) mod 32, d // 4 and its successor, each block 256 functions, indices taken modulo 8192; a list holds distinct indices. `point_counts`: some batch has all 512 points live in every draw.
All inputs are finite; a program needn't handle non-finite values.
Results may differ from the reference program's by a relative error of at most 0.006.
Values may be sent and summed in bfloat16 or wider, within the bound.
A program may use at most 64 MiB of HBM per device.

```python
import math
import jax
import jax.numpy as jnp
from jax import lax

NBF = 8192
NOCC = 2048
NLIST = 512
NPTS = 512
BATCH_DEV = 1
NBATCH = 128
TILE = 256
WIN = 768
N_ROW = 32
N_COL = 4


group_count = 8


common_gain = 2.8284271


def draw_point_counts(key, part):
    first_key, second_key = jax.random.split(key)
    levels = jax.random.randint(first_key, (NBATCH,), 1, NPTS + 1)
    position = jax.random.randint(second_key, (), 0, NBATCH)
    return levels.at[position].set(NPTS).astype(jnp.int32)


def draw_func_lists(key, part):
    keys_all = jax.random.split(key, NBATCH)

    def one_list(batch_key):
        picked = jax.random.permutation(batch_key, WIN - 3)[:NLIST - 3]
        mapped = jnp.where(picked + 1 < TILE - 1, picked + 1, picked + 2)
        fixed_ends = jnp.array([0, TILE - 1, WIN - 1], jnp.int32)
        return jnp.sort(jnp.concatenate([fixed_ends, mapped.astype(jnp.int32)]))
    offsets = jax.vmap(one_list)(keys_all)
    holder_row = jnp.arange(NBATCH, dtype=jnp.int32) // BATCH_DEV // N_COL
    first_func = (holder_row - 1) % N_ROW * TILE
    return ((first_func[:, None] + offsets) % NBF).astype(jnp.int32)


def draw_coeffs(key, part):
    common_key = jax.random.fold_in(key, 0)
    single_key = jax.random.fold_in(key, 1)
    group_key = jax.random.fold_in(key, 3)
    factor = (2.0 * NOCC) ** (-0.5)
    lead_orbitals = NOCC // 4
    groups = jax.random.randint(group_key, (NBF,), 0, group_count)
    orbital_gain = (jnp.arange(NOCC) < lead_orbitals).astype(jnp.float32) * common_gain
    common = jnp.clip(jax.random.normal(common_key, (group_count, NOCC), jnp.float32), -2.5, 2.5)
    single = jnp.clip(jax.random.normal(single_key, (NBF, NOCC), jnp.float32), -2.5, 2.5)
    values = jnp.take(common, groups, axis=0) * orbital_gain[None, :] + single
    return (factor * values).astype(jnp.bfloat16)


def draw_basis_values(key, part):
    noise_key, shared_key = jax.random.split(key, 2)
    spread = (2.0 * NLIST) ** (-0.5)
    shared_weight = (3.0 / NLIST) ** 0.5
    noise = jnp.clip(jax.random.normal(noise_key, (NBATCH, NPTS, NLIST), jnp.float32), -4.0, 4.0)
    shared = jnp.clip(jax.random.normal(shared_key, (NBATCH, NPTS, 1), jnp.float32), -3.0, 3.0)
    values = noise + shared_weight * shared
    return (spread * values).astype(jnp.bfloat16)


def block_levels(stream_key, dims, shards, low, largest):
    def one(axis_at, shards_of):
        steps = jax.random.uniform(jax.random.fold_in(jax.random.fold_in(stream_key, 6), axis_at), (shards_of,), jnp.float32, low / len(shards), largest / len(shards))
        return jnp.repeat(jnp.exp(steps), dims[axis_at] // shards_of).reshape((-1,) + (1,) * (len(dims) - axis_at - 1))

    gain = one(*shards[0])
    for cut in shards[1:]:
        gain = gain * one(*cut)
    return gain


def setup_inputs(seed: int = 0) -> dict:
    keys = jax.random.split(jax.random.key(seed), 6)
    coeffs = draw_coeffs(jax.random.fold_in(keys[5], 71), 0)
    basis_values = draw_basis_values(jax.random.fold_in(keys[5], 71), 0)
    point_weights = jnp.clip(jnp.exp(math.log(1.0) - 2.9957323 * jax.random.uniform(keys[2], (NBATCH, NPTS), jnp.float32) ** block_levels(keys[2], (NBATCH, NPTS), ((0, 128),), -0.2, 0.2)), 0.05, 1.0)
    point_counts = draw_point_counts(jax.random.fold_in(keys[5], 71), 0)
    func_lists = draw_func_lists(jax.random.fold_in(keys[5], 71), 0)
    return {"coeffs": coeffs, "basis_values": basis_values, "point_weights": point_weights, "point_counts": point_counts, "func_lists": func_lists}


slater_coef = 0.9847450218426965


def exchange_potential(density_pts):
    return -slater_coef * jnp.power(density_pts + 1.0, 1.0 / 3.0)


def reference(coeffs, basis_values, point_weights, point_counts, func_lists):
    density = (2.0 * jnp.dot(coeffs, coeffs.T, preferred_element_type=jnp.float32)).astype(jnp.bfloat16)

    def add_batch(summed, batch_item):
        basis_block, weights, count_pts, func_index = batch_item
        dens_block = density[func_index][:, func_index]
        projected = jnp.dot(basis_block, dens_block, preferred_element_type=jnp.float32)
        density_pts = jnp.sum(projected * basis_block.astype(jnp.float32), axis=1)
        is_live = jnp.arange(NPTS) < count_pts
        pot_pts = jnp.where(is_live, weights * exchange_potential(density_pts), jnp.float32(0.0))
        scaled = (basis_block.astype(jnp.float32) * pot_pts[:, None]).astype(jnp.bfloat16)
        pot_block = jnp.dot(basis_block.T, scaled, preferred_element_type=jnp.float32)
        return summed.at[func_index[:, None], func_index[None, :]].add(pot_block), None

    potential, _ = lax.scan(add_batch, jnp.zeros((NBF, NBF), jnp.float32), (basis_values, point_weights, point_counts, func_lists))
    return density, potential
```

```python
import functools
import jax
import jax.numpy as jnp
from jax import lax
from jax.experimental import pallas as pl
from jax.experimental.pallas import tpu as pltpu
from jax.sharding import PartitionSpec as P

slater_coef = 0.9847450218426965
MESH = pl.DeviceIdType.MESH
f32 = jnp.float32
bf16 = jnp.bfloat16

OFFSET = (-1, 1, 2, 0)
NT = (((1,), (1,)), ((), ()))


def kernel(
    c_ref, phi_ref, pack_ref, dens_ref, pot_ref,
    panel, slices, window, phis, packs, window_t, spread, scaled, rho_own, rho_in, v_out, v_in,
    ag_send, ag_recv, mate_send, mate_recv, z_send, z_recv, phi_send, phi_recv, pack_send, pack_recv,
    turn_send, win_send, win_recv, rho_send, rho_recv, v_send, v_recv, local_sem,
):
    row = lax.axis_index("row")
    z = lax.axis_index("col")
    k = lax.rem(row, 2)
    x = lax.rem(row // 2, 4)
    y = row // 8
    d = 1 - 2 * k
    diag = y == z
    off_diag = y != z

    def place(dx=0, dy=0, dz=0, core=None):
        xx = lax.rem(x + dx + 8, 4)
        yy = lax.rem(y + dy + 8, 4)
        core = k if core is None else core
        return ((yy * 4 + xx) * 2 + core, lax.rem(z + dz + 8, 4))

    def shifted(dr, dz):
        return (lax.rem(row + dr + 32, 32), lax.rem(z + dz + 4, 4))

    mate = place(core=1 - k)
    turn_to = ((lax.rem(2 * y - z + 8, 4) * 4 + x) * 2 + k, y)
    turn_from = ((z * 4 + x) * 2 + k, lax.rem(2 * z - y + 8, 4))
    holder = (row, y)

    barrier = pltpu.get_barrier_semaphore()
    friends = [mate, place(dx=1), place(dx=-1), place(dy=1), place(dy=-1), place(dz=2)]
    friends += [shifted(dr, dz) for dr in (-1, 0, 1) for dz in (-1, 0, 1) if dr or dz]
    for friend in friends:
        pl.semaphore_signal(barrier, inc=1, device_id=friend, device_id_type=MESH)

    @pl.when(off_diag)
    def _():
        for friend in (turn_to, turn_from):
            pl.semaphore_signal(barrier, inc=1, device_id=friend, device_id_type=MESH)

    pl.semaphore_wait(barrier, len(friends) + 2 * off_diag.astype(jnp.int32))

    sends = []

    def remote(src, dst, send_sem, recv_sem, device, keep=True):
        copy = pltpu.make_async_remote_copy(
            src_ref=src, dst_ref=dst, send_sem=send_sem, recv_sem=recv_sem,
            device_id=device, device_id_type=MESH,
        )
        if keep:
            copy.start()
            sends.append(copy)
        return copy

    def arrived(dst, recv_sem):
        pltpu.make_async_remote_copy(
            src_ref=dst, dst_ref=dst, send_sem=ag_send.at[0], recv_sem=recv_sem,
            device_id=mate, device_id_type=MESH,
        ).wait_recv()

    def piece(h, s1, s2, core=None):
        core_now, way = (k, d) if core is None else (1 - k, -d)
        first, second = (x, y) if h == 0 else (y, x)
        o1 = lax.rem(first + OFFSET[s1] * way + 8, 4)
        o2 = lax.rem(second + OFFSET[s2] * way + 8, 4)
        sx, sy = (o1, o2) if h == 0 else (o2, o1)
        return panel.at[sx * 2 + core_now, lax.rem(2 * z - sy + 8, 4), pl.ds(h * 128, 128)]

    def ring(h, stage, step):
        along_x = (h == 0) == (stage == 1)
        return place(dx=step) if along_x else place(dy=step)

    counter = [0]

    def ag(h, s1, s2, to1, to2, device):
        ref = piece(h, s1, s2)
        remote(ref, ref, ag_send.at[counter[0]], ag_recv.at[h, to1, to2], device)
        counter[0] += 1

    def ag_first(h):
        ag(h, 3, 3, 0, 3, ring(h, 1, d))
        ag(h, 3, 3, 1, 3, ring(h, 1, -d))

    def ag_second(h, s1):
        ag(h, s1, 3, s1, 0, ring(h, 2, d))
        ag(h, s1, 3, s1, 1, ring(h, 2, -d))

    def to_mate(h, s1, s2):
        ref = piece(h, s1, s2)
        remote(ref, ref, mate_send.at[h, s1, s2], mate_recv.at[h, s1, s2], mate)

    def ag_wait(h, s1, s2):
        arrived(piece(h, s1, s2), ag_recv.at[h, s1, s2])
        to_mate(h, s1, s2)

    own_piece = panel.at[x * 2 + k, z]

    @pl.when(off_diag)
    def _():
        for h in range(2):
            part = pl.ds(h * 128, 128)
            remote(
                c_ref.at[part], own_piece.at[part], turn_send.at[h], ag_recv.at[h, 3, 3], turn_to, keep=False
            ).start()

    @pl.when(diag)
    def _():
        pltpu.make_async_copy(c_ref, own_piece, local_sem).start()

    for side, dr in ((0, 1), (1, -1)):
        remote(c_ref, window.at[side], win_send.at[side], win_recv.at[side], shifted(dr, 0))
    remote(pack_ref, packs.at[0], pack_send.at[0], pack_recv.at[0], place(dz=d))
    remote(pack_ref, packs.at[1], pack_send.at[1], pack_recv.at[1], place(dz=-d))

    def phi_part(chunk):
        return pl.ds(chunk * 256, 256)

    for chunk in range(2):
        for slot, way in ((0, d), (1, -d)):
            remote(
                phi_ref.at[phi_part(chunk)], phis.at[slot, phi_part(chunk)],
                phi_send.at[slot, chunk], phi_recv.at[slot, chunk], place(dz=way),
            )

    def phi_relay(chunk):
        ref = phis.at[0, phi_part(chunk)]
        arrived(ref, phi_recv.at[0, chunk])
        remote(ref, phis.at[2, phi_part(chunk)], phi_send.at[2, chunk], phi_recv.at[2, chunk], place(dz=d))

    def phi_wait(slot, chunk):
        arrived(phis.at[slot, phi_part(chunk)], phi_recv.at[slot, chunk])

    def pack_relay():
        arrived(packs.at[0], pack_recv.at[0])
        remote(packs.at[0], packs.at[2], pack_send.at[2], pack_recv.at[2], place(dz=d))

    def z_first():
        remote(c_ref, slices.at[0], z_send.at[0], z_recv.at[0], place(dz=d))
        remote(c_ref, slices.at[1], z_send.at[1], z_recv.at[1], place(dz=-d))

    def z_relay():
        arrived(slices.at[0], z_recv.at[0])
        remote(slices.at[0], slices.at[2], z_send.at[2], z_recv.at[2], place(dz=d))

    def zero_fill():
        pot_ref[...] = jnp.zeros_like(pot_ref)

    def spread_batch(slot):
        ref, pack = (phi_ref, pack_ref) if slot == 3 else (phis.at[slot], packs.at[slot])
        index = pack[0:1, :]
        slots = lax.broadcasted_iota(jnp.int32, (768, 512), 0).astype(f32)
        selector = jnp.where(slots == index, 1.0, 0.0).astype(bf16)
        spread[slot] = lax.dot_general(selector, ref[...], NT, preferred_element_type=f32).astype(bf16)

    def batch_of(slot):
        return lax.rem(z + OFFSET[slot] * d + 8, 4)

    def partial_rho(slot):
        mixed = jnp.dot(window_t[...], spread[slot], preferred_element_type=f32)
        rho_own[batch_of(slot)] = 2.0 * jnp.sum(mixed * mixed, axis=0, keepdims=True)

    def turn_window(side):
        if side == 1:
            window_t[:, 256:512] = c_ref[...].T
        else:
            index = side // 2
            arrived(window.at[index], win_recv.at[index])
            window_t[:, side * 256 : side * 256 + 256] = window[index].T

    spread_batch(3)
    turn_window(1)
    zero_fill()

    @pl.when(off_diag)
    def _():
        arrived(piece(0, 3, 3), ag_recv.at[0, 3, 3])

    @pl.when(diag)
    def _():
        pltpu.make_async_copy(c_ref, own_piece, local_sem).wait()

    ag_first(0)

    @pl.when(off_diag)
    def _():
        arrived(piece(1, 3, 3), ag_recv.at[1, 3, 3])

    ag_first(1)
    ag_second(0, 3)
    ag_second(1, 3)
    to_mate(0, 3, 3)
    to_mate(1, 3, 3)
    pack_relay()
    turn_window(0)
    turn_window(2)
    partial_rho(3)

    def stage_one(h, s1):
        ag_wait(h, s1, 3)
        if s1 == 0:
            ag(h, 0, 3, 2, 3, ring(h, 1, d))
        ag_second(h, s1)

    def stage_two(h, s1, s2):
        ag_wait(h, s1, s2)
        if s2 == 0:
            ag(h, s1, 0, s1, 2, ring(h, 2, d))

    stage_one(0, 0)
    stage_one(1, 0)
    stage_one(0, 1)
    stage_one(1, 1)
    phi_relay(0)
    stage_one(0, 2)
    stage_one(1, 2)
    for h in range(2):
        stage_two(h, 3, 0)
    phi_relay(1)
    z_first()
    for h in range(2):
        stage_two(h, 3, 1)
    arrived(packs.at[1], pack_recv.at[1])
    arrived(packs.at[2], pack_recv.at[2])
    spread_batch(0)
    for h in range(2):
        stage_two(h, 0, 0)
    partial_rho(0)
    for h in range(2):
        stage_two(h, 0, 1)
    phi_wait(1, 0)
    phi_wait(1, 1)
    spread_batch(1)
    for h in range(2):
        stage_two(h, 1, 0)
    partial_rho(1)
    for h in range(2):
        stage_two(h, 1, 1)
        stage_two(h, 2, 0)
    phi_wait(2, 0)
    phi_wait(2, 1)
    z_relay()
    spread_batch(2)
    partial_rho(2)

    from_holder = lax.rem(z - y + 4, 4)

    @pl.when(off_diag)
    def _():
        remote(
            rho_own, rho_in.at[from_holder], rho_send, rho_recv.at[from_holder], holder, keep=False
        ).start()

    for h in range(2):
        stage_two(h, 2, 1)
        for s1 in (3, 0, 1, 2):
            stage_two(h, s1, 2)

    strips = (2 * k, 2 - 2 * k, 1)

    def block_place(strip, t):
        column = lax.rem(row + strip - 1 + 32, 32)
        line = lax.rem(row + t - 1 + 32, 32)
        return column, line

    def v_copy(strip, order, t):
        column, line = block_place(strip, t)
        return remote(
            v_out.at[order, t], v_in.at[2 - strip, t], v_send.at[order, t], v_recv.at[2 - strip, t],
            (column, line // 8), keep=False,
        )

    @pl.when(diag)
    def _():
        for o in (1, 2, 3):
            arrived(rho_in.at[o], rho_recv.at[o])
        for slot in range(4):
            b = batch_of(slot)
            rho = rho_own[b] + rho_in[1, b] + rho_in[2, b] + rho_in[3, b]
            pack = pack_ref if slot == 3 else packs.at[slot]
            pot = pack[1:2, :] * (-slater_coef * jnp.exp(jnp.log(rho + 1.0) * (1.0 / 3.0)))
            scaled[slot] = (spread[slot].astype(f32) * pot).astype(bf16)
        for order in range(3):
            strip = strips[order]
            for t in range(3):
                total = jnp.zeros((256, 256), f32)
                for slot in range(4):
                    total += lax.dot_general(
                        spread[slot, t * 256 : t * 256 + 256],
                        scaled[slot, pl.ds(pl.multiple_of(strip * 256, 256), 256)],
                        NT, preferred_element_type=f32,
                    )
                if order < 2:
                    v_out[order, t] = total.astype(bf16)
                    v_copy(strip, order, t).start()
                else:
                    _, line = block_place(1, t)
                    if t == 1:
                        pot_ref[pl.ds(pl.multiple_of(lax.rem(line, 8) * 256, 256), 256), :] += total
                    else:

                        @pl.when(line // 8 == z)
                        def _():
                            pot_ref[pl.ds(pl.multiple_of(lax.rem(line, 8) * 256, 256), 256), :] += total

                        @pl.when(line // 8 != z)
                        def _():
                            v_out[order, t] = total.astype(bf16)
                            v_copy(1, order, t).start()

    z_order = (3, 0, 1, 2)
    arrived(slices.at[1], z_recv.at[1])
    arrived(slices.at[2], z_recv.at[2])
    for h in range(2):
        for s1 in range(4):
            for s2 in range(4):
                arrived(piece(h, s1, s2, core=1), mate_recv.at[h, s1, s2])

    def density_block(block, carry):
        total = jnp.zeros((256, 256), f32)
        for slot in z_order:
            mine = c_ref[...] if slot == 3 else slices[slot]
            total += lax.dot_general(panel[block, batch_of(slot)], mine, NT, preferred_element_type=f32)
        dens_ref[pl.ds(pl.multiple_of(block * 256, 256), 256), :] = (2.0 * total).astype(bf16)
        return carry

    lax.fori_loop(0, 8, density_block, 0)

    for s in range(3):
        for t in range(3):
            source = lax.rem(row + s - 1 + 32, 32)
            line = lax.rem(source + t - 1 + 32, 32)
            coming = line // 8 == z
            if s == 1:
                coming = jnp.logical_and(coming, source // 8 != z)

            @pl.when(coming)
            def _():
                arrived(v_in.at[s, t], v_recv.at[s, t])
                pot_ref[pl.ds(pl.multiple_of(lax.rem(line, 8) * 256, 256), 256), :] += v_in[s, t].astype(f32)

    for copy in sends:
        copy.wait_send()

    @pl.when(off_diag)
    def _():
        for h in range(2):
            part = pl.ds(h * 128, 128)
            remote(
                c_ref.at[part], own_piece.at[part], turn_send.at[h], ag_recv.at[h, 3, 3], turn_to, keep=False
            ).wait_send()
        remote(
            rho_own, rho_in.at[from_holder], rho_send, rho_recv.at[from_holder], holder, keep=False
        ).wait_send()

    @pl.when(diag)
    def _():
        for order in range(3):
            for t in range(3):
                if order < 2:
                    v_copy(strips[order], order, t).wait_send()
                elif t != 1:
                    _, line = block_place(1, t)

                    @pl.when(line // 8 != z)
                    def _():
                        v_copy(1, order, t).wait_send()


def on_device(coeffs, basis_values, point_weights, point_counts, func_lists):
    row = lax.axis_index("row")
    window_start = ((row + 31) % 32) * 256
    index = ((func_lists[0] - window_start + 8192) % 8192).astype(f32)
    weights = jnp.where(jnp.arange(512, dtype=jnp.int32) < point_counts[0], point_weights[0], 0.0)
    line = lax.broadcasted_iota(jnp.int32, (8, 512), 0)
    pack = jnp.where(line == 0, index[None, :], jnp.where(line == 1, weights[None, :], 0.0))
    dma = pltpu.SemaphoreType.DMA
    density, potential = pl.pallas_call(
        kernel,
        out_shape=(
            jax.ShapeDtypeStruct((2048, 256), bf16),
            jax.ShapeDtypeStruct((2048, 256), f32),
        ),
        in_specs=[pl.BlockSpec(memory_space=pltpu.VMEM)] * 3,
        out_specs=(pl.BlockSpec(memory_space=pltpu.VMEM),) * 2,
        scratch_shapes=[
            pltpu.VMEM((8, 4, 256, 512), bf16),
            pltpu.VMEM((3, 256, 512), bf16),
            pltpu.VMEM((2, 256, 512), bf16),
            pltpu.VMEM((3, 512, 512), bf16),
            pltpu.VMEM((3, 8, 512), f32),
            pltpu.VMEM((512, 768), bf16),
            pltpu.VMEM((4, 768, 512), bf16),
            pltpu.VMEM((4, 768, 512), bf16),
            pltpu.VMEM((4, 1, 512), f32),
            pltpu.VMEM((4, 4, 1, 512), f32),
            pltpu.VMEM((3, 3, 256, 256), bf16),
            pltpu.VMEM((3, 3, 256, 256), bf16),
            dma((30,)), dma((2, 4, 4)), dma((2, 4, 4)), dma((2, 4, 4)),
            dma((3,)), dma((3,)), dma((3, 2)), dma((3, 2)), dma((3,)), dma((3,)),
            dma((2,)), dma((2,)), dma((2,)), dma, dma((4,)), dma((3, 3)), dma((3, 3)), dma,
        ],
        compiler_params=pltpu.CompilerParams(
            collective_id=0, has_side_effects=True, vmem_limit_bytes=60000 * 1024
        ),
    )(coeffs, basis_values.reshape(512, 512), pack)
    return density, potential


def solution(mesh):
    in_specs = (
        P("row", "col"),
        P(("row", "col"), None, None),
        P(("row", "col"), None),
        P(("row", "col")),
        P(("row", "col"), None),
    )
    out_specs = (P("col", "row"), P("col", "row"))
    return jax.shard_map(
        on_device, mesh=mesh, in_specs=in_specs, out_specs=out_specs, check_vma=False
    )
```

```python
import functools
import jax
import jax.numpy as jnp
from jax import lax
from jax.experimental import pallas as pl
from jax.experimental.pallas import tpu as pltpu
from jax.sharding import PartitionSpec as P

slater_coef = 0.9847450218426965
MESH = pl.DeviceIdType.MESH
f32 = jnp.float32
bf16 = jnp.bfloat16

OFFSET = (-1, 1, 2, 0)
NT = (((1,), (1,)), ((), ()))


def kernel(
    count_ref, c_hbm, phi_hbm, list_hbm, weight_hbm, dens_ref, pot_ref,
    c_ref, phi_ref, list_ref, weight_ref,
    panel, slices, window, phis, packs, window_t, selectors, spread, scaled, rho_own, rho_in, v_out, v_in,
    ag_send, ag_recv, mate_send, mate_recv, z_send, z_recv, phi_send, phi_recv, pack_send, pack_recv,
    turn_send, win_send, win_recv, rho_send, rho_recv, v_send, v_recv, local_sem, load_sem,
):
    row = lax.axis_index("row")
    z = lax.axis_index("col")
    k = lax.rem(row, 2)
    x = lax.rem(row // 2, 4)
    y = row // 8
    d = 1 - 2 * k
    diag = y == z
    off_diag = y != z

    def place(dx=0, dy=0, dz=0, core=None):
        xx = lax.rem(x + dx + 8, 4)
        yy = lax.rem(y + dy + 8, 4)
        core = k if core is None else core
        return ((yy * 4 + xx) * 2 + core, lax.rem(z + dz + 8, 4))

    def shifted(dr, dz):
        return (lax.rem(row + dr + 32, 32), lax.rem(z + dz + 4, 4))

    mate = place(core=1 - k)
    turn_to = ((lax.rem(2 * y - z + 8, 4) * 4 + x) * 2 + k, y)
    turn_from = ((z * 4 + x) * 2 + k, lax.rem(2 * z - y + 8, 4))
    holder = (row, y)

    loads = [
        pltpu.make_async_copy(source, target, load_sem.at[i])
        for i, (source, target) in enumerate(
            ((list_hbm, list_ref), (weight_hbm, weight_ref), (phi_hbm, phi_ref), (c_hbm, c_ref))
        )
    ]
    for load in loads:
        load.start()
    barrier = pltpu.get_barrier_semaphore()
    friends = [mate, place(dx=1), place(dx=-1), place(dy=1), place(dy=-1), place(dz=2)]
    friends += [shifted(dr, dz) for dr in (-1, 0, 1) for dz in (-1, 0, 1) if dr or dz]
    for friend in friends:
        pl.semaphore_signal(barrier, inc=1, device_id=friend, device_id_type=MESH)

    @pl.when(off_diag)
    def _():
        for friend in (turn_to, turn_from):
            pl.semaphore_signal(barrier, inc=1, device_id=friend, device_id_type=MESH)

    sends = []

    def remote(src, dst, send_sem, recv_sem, device, keep=True):
        copy = pltpu.make_async_remote_copy(
            src_ref=src, dst_ref=dst, send_sem=send_sem, recv_sem=recv_sem,
            device_id=device, device_id_type=MESH,
        )
        if keep:
            copy.start()
            sends.append(copy)
        return copy

    def arrived(dst, recv_sem):
        pltpu.make_async_remote_copy(
            src_ref=dst, dst_ref=dst, send_sem=ag_send.at[0], recv_sem=recv_sem,
            device_id=mate, device_id_type=MESH,
        ).wait_recv()

    def piece(h, s1, s2, core=None):
        core_now, way = (k, d) if core is None else (1 - k, -d)
        first, second = (x, y) if h == 0 else (y, x)
        o1 = lax.rem(first + OFFSET[s1] * way + 8, 4)
        o2 = lax.rem(second + OFFSET[s2] * way + 8, 4)
        sx, sy = (o1, o2) if h == 0 else (o2, o1)
        return panel.at[sx * 2 + core_now, lax.rem(2 * z - sy + 8, 4), pl.ds(h * 128, 128)]

    def ring(h, stage, step):
        along_x = (h == 0) == (stage == 1)
        return place(dx=step) if along_x else place(dy=step)

    counter = [0]

    def ag(h, s1, s2, to1, to2, device):
        ref = piece(h, s1, s2)
        remote(ref, ref, ag_send.at[counter[0]], ag_recv.at[h, to1, to2], device)
        counter[0] += 1

    def ag_first(h):
        ag(h, 3, 3, 0, 3, ring(h, 1, d))
        ag(h, 3, 3, 1, 3, ring(h, 1, -d))

    def ag_second(h, s1):
        ag(h, s1, 3, s1, 0, ring(h, 2, d))
        ag(h, s1, 3, s1, 1, ring(h, 2, -d))

    def to_mate(h, s1, s2):
        ref = piece(h, s1, s2)
        remote(ref, ref, mate_send.at[h, s1, s2], mate_recv.at[h, s1, s2], mate)

    def ag_wait(h, s1, s2):
        arrived(piece(h, s1, s2), ag_recv.at[h, s1, s2])
        to_mate(h, s1, s2)

    own_piece = panel.at[x * 2 + k, z]
    pack_ref = packs.at[3]

    def phi_part(chunk):
        return pl.ds(chunk * 128, 128)

    def phi_first(chunk):
        for slot, way in ((0, d), (1, -d)):
            remote(
                phi_ref.at[phi_part(chunk)], phis.at[slot, phi_part(chunk)],
                phi_send.at[slot, chunk], phi_recv.at[slot, chunk], place(dz=way),
            )

    def phi_relay(chunk):
        ref = phis.at[0, phi_part(chunk)]
        arrived(ref, phi_recv.at[0, chunk])
        remote(ref, phis.at[2, phi_part(chunk)], phi_send.at[2, chunk], phi_recv.at[2, chunk], place(dz=d))

    def phi_wait(slot, chunk):
        arrived(phis.at[slot, phi_part(chunk)], phi_recv.at[slot, chunk])

    def pack_first():
        remote(pack_ref, packs.at[0], pack_send.at[0], pack_recv.at[0], place(dz=d))
        remote(pack_ref, packs.at[1], pack_send.at[1], pack_recv.at[1], place(dz=-d))

    def pack_relay():
        arrived(packs.at[0], pack_recv.at[0])
        remote(packs.at[0], packs.at[2], pack_send.at[2], pack_recv.at[2], place(dz=d))
        arrived(packs.at[1], pack_recv.at[1])

    def z_first():
        remote(c_ref, slices.at[0], z_send.at[0], z_recv.at[0], place(dz=d))
        remote(c_ref, slices.at[1], z_send.at[1], z_recv.at[1], place(dz=-d))

    def z_relay():
        arrived(slices.at[0], z_recv.at[0])
        remote(slices.at[0], slices.at[2], z_send.at[2], z_recv.at[2], place(dz=d))

    def pack_own():
        window_start = lax.rem(row + 31, 32) * 256
        index = list_ref[...] - window_start
        packs[3, 0:1, :] = jnp.where(index < 0, index + 8192, index).astype(f32)
        point = lax.broadcasted_iota(jnp.int32, (1, 512), 1)
        packs[3, 1:2, :] = jnp.where(point < count_ref[0], weight_ref[...], 0.0)

    def zero_fill():
        pot_ref[...] = jnp.zeros_like(pot_ref)

    def select(slot):
        if slot == 2:
            arrived(packs.at[2], pack_recv.at[2])
        index = packs[slot, 0:1, :]
        slots = lax.broadcasted_iota(jnp.int32, (768, 512), 0).astype(f32)
        selectors[slot] = jnp.where(slots == index, 1.0, 0.0).astype(bf16)

    def spread_batch(slot):
        ref = phi_ref if slot == 3 else phis.at[slot]
        spread[:, slot * 512 : slot * 512 + 512] = lax.dot_general(
            selectors[slot], ref[...], NT, preferred_element_type=f32
        ).astype(bf16)

    def batch_of(slot):
        return lax.rem(z + OFFSET[slot] * d + 8, 4)

    def partial_rho(slot):
        mixed = jnp.dot(
            window_t[...], spread[:, slot * 512 : slot * 512 + 512], preferred_element_type=f32
        )
        rho_own[batch_of(slot)] = 2.0 * jnp.sum(mixed * mixed, axis=0, keepdims=True)

    def turn_window(side):
        if side == 1:
            window_t[:, 256:512] = c_ref[...].T
        else:
            index = side // 2
            arrived(window.at[index], win_recv.at[index])
            window_t[:, side * 256 : side * 256 + 256] = window[index].T

    def use(slot):
        if slot:
            for chunk in range(4):
                phi_wait(slot, chunk)
        spread_batch(slot)
        partial_rho(slot)

    zero_fill()
    loads[0].wait()
    loads[1].wait()
    pack_own()
    select(3)
    loads[2].wait()
    spread_batch(3)
    loads[3].wait()
    turn_window(1)
    pl.semaphore_wait(barrier, len(friends) + 2 * off_diag.astype(jnp.int32))

    @pl.when(off_diag)
    def _():
        for h in range(2):
            part = pl.ds(h * 128, 128)
            remote(
                c_ref.at[part], own_piece.at[part], turn_send.at[h], ag_recv.at[h, 3, 3], turn_to, keep=False
            ).start()

    @pl.when(diag)
    def _():
        pltpu.make_async_copy(c_ref, own_piece, local_sem).start()

    pack_first()

    def window_first():
        for side, dr in ((0, 1), (1, -1)):
            remote(c_ref, window.at[side], win_send.at[side], win_recv.at[side], shifted(dr, 0))

    def turn_wait(h):
        @pl.when(off_diag)
        def _():
            arrived(piece(h, 3, 3), ag_recv.at[h, 3, 3])

        if h == 0:

            @pl.when(diag)
            def _():
                pltpu.make_async_copy(c_ref, own_piece, local_sem).wait()

    def stage_one(h, s1):
        ag_wait(h, s1, 3)
        if s1 == 0:
            ag(h, 0, 3, 2, 3, ring(h, 1, d))

    def stage_two(h, s1, s2):
        ag_wait(h, s1, s2)
        if s2 == 0:
            ag(h, s1, 0, s1, 2, ring(h, 2, d))

    from_holder = lax.rem(z - y + 4, 4)

    def rho_out():
        @pl.when(off_diag)
        def _():
            remote(
                rho_own, rho_in.at[from_holder], rho_send, rho_recv.at[from_holder], holder, keep=False
            ).start()

    strips = (2 * k, 2 - 2 * k, 1)

    def block_place(strip, t):
        column = lax.rem(row + strip - 1 + 32, 32)
        line = lax.rem(row + t - 1 + 32, 32)
        return column, line

    def v_copy(strip, t):
        column, line = block_place(strip, t)
        return remote(
            v_out.at[strip, t], v_in.at[2 - strip, t], v_send.at[strip, t], v_recv.at[2 - strip, t],
            (column, line // 8), keep=False,
        )

    def window_sum():
        pl.when(diag)(window_sum_here)

    def window_sum_here():
        for o in (1, 2, 3):
            arrived(rho_in.at[o], rho_recv.at[o])
        for slot in range(4):
            b = batch_of(slot)
            rho = rho_own[b] + rho_in[1, b] + rho_in[2, b] + rho_in[3, b]
            pot = packs[slot, 1:2, :] * (-slater_coef * jnp.exp(jnp.log(rho + 1.0) * (1.0 / 3.0)))
            start = slot * 512
            scaled[:, start : start + 512] = (spread[:, start : start + 512].astype(f32) * pot).astype(bf16)
        sides = []
        for order in range(2):
            strip = strips[order]
            rows = scaled[pl.ds(pl.multiple_of(strip * 256, 256), 256), :]
            halves = [
                lax.dot_general(spread[i * 384 : i * 384 + 384], rows, NT, preferred_element_type=f32)
                for i in range(2)
            ]
            side = jnp.concatenate(halves, axis=0)
            sides.append(side[256:512])
            for t in range(3):
                v_out[strip, t] = side[t * 256 : t * 256 + 256].astype(bf16)
                v_copy(strip, t).start()
        centre = lax.dot_general(spread[256:512], scaled[256:512], NT, preferred_element_type=f32)
        for order, strip in ((2, 1), (0, strips[0]), (1, strips[1])):
            total = centre if order == 2 else sides[order].T
            _, line = block_place(1, strip)
            rows = pl.ds(pl.multiple_of(lax.rem(line, 8) * 256, 256), 256)
            if order == 2:
                pot_ref[rows, :] += total
            else:

                @pl.when(line // 8 == z)
                def _():
                    pot_ref[rows, :] += total

                @pl.when(line // 8 != z)
                def _():
                    v_out[1, strip] = total.astype(bf16)
                    v_copy(1, strip).start()

    steps = [
        (phi_first, 0), (phi_first, 1),
        (turn_wait, 0), (ag_first, 0), (phi_first, 2), (phi_first, 3),
        (turn_wait, 1), (ag_first, 1), (ag_second, 0, 3), (ag_second, 1, 3),
        (window_first,), (to_mate, 0, 3, 3), (to_mate, 1, 3, 3), (pack_relay,), (select, 0),
        (phi_relay, 0), (stage_one, 0, 0),
        (stage_one, 1, 0), (phi_relay, 1), (ag_second, 0, 0), (ag_second, 1, 0),
        (stage_one, 0, 1), (ag_second, 0, 1), (stage_one, 1, 1), (ag_second, 1, 1), (phi_relay, 2),
        (stage_two, 1, 3, 0), (stage_two, 0, 3, 0), (select, 1),
        (stage_one, 0, 2), (ag_second, 0, 2), (phi_relay, 3), (z_first,), (stage_one, 1, 2), (ag_second, 1, 2),
        (turn_window, 0), (turn_window, 2), (partial_rho, 3), (select, 2),
        (stage_two, 1, 0, 0), (stage_two, 0, 0, 0), (use, 0),
        (stage_two, 1, 1, 0), (use, 1), (stage_two, 0, 1, 0),
        (use, 2), (rho_out,), (stage_two, 1, 2, 0), (z_relay,), (stage_two, 0, 2, 0),
        (stage_two, 0, 3, 1), (stage_two, 1, 3, 1), (stage_two, 0, 0, 1), (stage_two, 1, 0, 1),
        (window_sum,),
        (stage_two, 0, 1, 1), (stage_two, 1, 1, 1), (stage_two, 0, 3, 2), (stage_two, 1, 3, 2),
        (stage_two, 0, 2, 1), (stage_two, 1, 2, 1), (stage_two, 0, 0, 2), (stage_two, 1, 0, 2),
        (stage_two, 0, 1, 2), (stage_two, 1, 1, 2), (stage_two, 0, 2, 2), (stage_two, 1, 2, 2),
    ]
    for call, *args in steps:
        call(*args)

    z_order = (3, 0, 1, 2)
    arrived(slices.at[1], z_recv.at[1])
    arrived(slices.at[2], z_recv.at[2])
    for h in range(2):
        for s1 in range(4):
            for s2 in range(4):
                arrived(piece(h, s1, s2, core=1), mate_recv.at[h, s1, s2])

    def density_pair(pair, carry):
        totals = [jnp.zeros((256, 256), f32) for _ in range(2)]
        for slot in z_order:
            mine = c_ref[...] if slot == 3 else slices[slot]
            for i in range(2):
                totals[i] += lax.dot_general(
                    panel[2 * pair + i, batch_of(slot)], mine, NT, preferred_element_type=f32
                )
        for i in range(2):
            dens_ref[pl.ds(pl.multiple_of((2 * pair + i) * 256, 256), 256), :] = (2.0 * totals[i]).astype(bf16)
        return carry

    lax.fori_loop(0, 4, density_pair, 0)

    for s in range(3):
        for t in range(3):
            source = lax.rem(row + s - 1 + 32, 32)
            line = lax.rem(source + t - 1 + 32, 32)
            coming = line // 8 == z
            if s == 1:
                coming = jnp.logical_and(coming, source // 8 != z)

            @pl.when(coming)
            def _():
                arrived(v_in.at[s, t], v_recv.at[s, t])
                pot_ref[pl.ds(pl.multiple_of(lax.rem(line, 8) * 256, 256), 256), :] += v_in[s, t].astype(f32)

    for copy in sends:
        copy.wait_send()

    @pl.when(off_diag)
    def _():
        for h in range(2):
            part = pl.ds(h * 128, 128)
            remote(
                c_ref.at[part], own_piece.at[part], turn_send.at[h], ag_recv.at[h, 3, 3], turn_to, keep=False
            ).wait_send()
        remote(
            rho_own, rho_in.at[from_holder], rho_send, rho_recv.at[from_holder], holder, keep=False
        ).wait_send()

    @pl.when(diag)
    def _():
        for order in range(3):
            for t in range(3):
                if order < 2:
                    v_copy(strips[order], t).wait_send()
                elif t != 1:
                    _, line = block_place(1, t)

                    @pl.when(line // 8 != z)
                    def _():
                        v_copy(1, t).wait_send()


def on_device(coeffs, basis_values, point_weights, point_counts, func_lists):
    dma = pltpu.SemaphoreType.DMA
    density, potential = pl.pallas_call(
        kernel,
        out_shape=(
            pltpu.VMEM((2048, 256), bf16),
            pltpu.VMEM((2048, 256), f32),
        ),
        in_specs=[pl.BlockSpec(memory_space=pltpu.SMEM)] + [pl.BlockSpec(memory_space=pltpu.HBM)] * 4,
        out_specs=(pl.BlockSpec(memory_space=pltpu.VMEM),) * 2,
        scratch_shapes=[
            pltpu.VMEM((256, 512), bf16),
            pltpu.VMEM((512, 512), bf16),
            pltpu.VMEM((1, 512), jnp.int32),
            pltpu.VMEM((1, 512), f32),
            pltpu.VMEM((8, 4, 256, 512), bf16),
            pltpu.VMEM((3, 256, 512), bf16),
            pltpu.VMEM((2, 256, 512), bf16),
            pltpu.VMEM((3, 512, 512), bf16),
            pltpu.VMEM((4, 8, 512), f32),
            pltpu.VMEM((512, 768), bf16),
            pltpu.VMEM((4, 768, 512), bf16),
            pltpu.VMEM((768, 2048), bf16),
            pltpu.VMEM((768, 2048), bf16),
            pltpu.VMEM((4, 1, 512), f32),
            pltpu.VMEM((4, 4, 1, 512), f32),
            pltpu.VMEM((3, 3, 256, 256), bf16),
            pltpu.VMEM((3, 3, 256, 256), bf16),
            dma((30,)), dma((2, 4, 4)), dma((2, 4, 4)), dma((2, 4, 4)),
            dma((3,)), dma((3,)), dma((3, 4)), dma((3, 4)), dma((3,)), dma((3,)),
            dma((2,)), dma((2,)), dma((2,)), dma, dma((4,)), dma((3, 3)), dma((3, 3)), dma, dma((4,)),
        ],
        compiler_params=pltpu.CompilerParams(
            collective_id=0, has_side_effects=True, vmem_limit_bytes=36 * 1024 * 1024
        ),
    )(
        point_counts,
        *(
            pltpu.with_memory_space_constraint(array, pltpu.HBM)
            for array in (coeffs, basis_values.reshape(512, 512), func_lists, point_weights)
        ),
    )
    return density, potential


def solution(mesh):
    in_specs = (
        P("row", "col"),
        P(("row", "col"), None, None),
        P(("row", "col"), None),
        P(("row", "col")),
        P(("row", "col"), None),
    )
    out_specs = (P("col", "row"), P("col", "row"))
    return jax.shard_map(
        on_device, mesh=mesh, in_specs=in_specs, out_specs=out_specs, check_vma=False
    )
```

```python
import functools
import jax
import jax.numpy as jnp
from jax import lax
from jax.experimental import pallas as pl
from jax.experimental.pallas import tpu as pltpu
from jax.sharding import PartitionSpec as P

slater_coef = 0.9847450218426965
MESH = pl.DeviceIdType.MESH
f32 = jnp.float32
bf16 = jnp.bfloat16

OFFSET = (-1, 1, 2, 0)
NT = (((1,), (1,)), ((), ()))


def kernel(
    count_ref, c_hbm, phi_hbm, list_hbm, weight_hbm, dens_ref, pot_ref,
    c_ref, phi_ref, list_ref, weight_ref,
    panel, slices, window, phis, packs, window_t, selectors, spread, scaled, rho_own, rho_in, crossing, pots, dens_sum, v_out, v_in,
    ag_send, ag_recv, mate_send, mate_recv, z_send, z_recv, phi_send, phi_recv, phi_rest, pack_send, pack_recv,
    turn_send, win_send, win_recv, rho_send, rho_recv, v_send, v_recv, local_sem, load_sem,
):
    row = lax.axis_index("row")
    z = lax.axis_index("col")
    k = lax.rem(row, 2)
    x = lax.rem(row // 2, 4)
    y = row // 8
    d = 1 - 2 * k
    diag = y == z
    off_diag = y != z

    def place(dx=0, dy=0, dz=0, core=None):
        xx = lax.rem(x + dx + 8, 4)
        yy = lax.rem(y + dy + 8, 4)
        core = k if core is None else core
        return ((yy * 4 + xx) * 2 + core, lax.rem(z + dz + 8, 4))

    def shifted(dr, dz):
        return (lax.rem(row + dr + 32, 32), lax.rem(z + dz + 4, 4))

    mate = place(core=1 - k)
    turn_to = ((lax.rem(2 * y - z + 8, 4) * 4 + x) * 2 + k, y)
    turn_from = ((z * 4 + x) * 2 + k, lax.rem(2 * z - y + 8, 4))
    holder = (row, y)

    loads = [
        pltpu.make_async_copy(source, target, load_sem.at[i])
        for i, (source, target) in enumerate(
            ((list_hbm, list_ref), (weight_hbm, weight_ref), (phi_hbm, phi_ref), (c_hbm, c_ref))
        )
    ]
    for load in loads:
        load.start()
    barrier = pltpu.get_barrier_semaphore()
    friends = [mate, place(dx=1), place(dx=-1), place(dy=1), place(dy=-1), place(dz=2)]
    friends += [shifted(dr, dz) for dr in (-1, 0, 1) for dz in (-1, 0, 1) if dr or dz]
    for friend in friends:
        pl.semaphore_signal(barrier, inc=1, device_id=friend, device_id_type=MESH)

    @pl.when(off_diag)
    def _():
        for friend in (turn_to, turn_from):
            pl.semaphore_signal(barrier, inc=1, device_id=friend, device_id_type=MESH)

    def remote(src, dst, send_sem, recv_sem, device, keep=True):
        copy = pltpu.make_async_remote_copy(
            src_ref=src, dst_ref=dst, send_sem=send_sem, recv_sem=recv_sem,
            device_id=device, device_id_type=MESH,
        )
        if keep:
            copy.start()
        return copy

    def arrived(dst, recv_sem):
        pltpu.make_async_remote_copy(
            src_ref=dst, dst_ref=dst, send_sem=mate_send, recv_sem=recv_sem,
            device_id=mate, device_id_type=MESH,
        ).wait_recv()

    def piece(h, s1, s2, core=None):
        core_now, way = (k, d) if core is None else (1 - k, -d)
        first, second = (x, y) if h == 0 else (y, x)
        o1 = lax.rem(first + OFFSET[s1] * way + 8, 4)
        o2 = lax.rem(second + OFFSET[s2] * way + 8, 4)
        sx, sy = (o1, o2) if h == 0 else (o2, o1)
        return panel.at[sx * 2 + core_now, lax.rem(2 * z - sy + 8, 4), pl.ds(h * 128, 128)]

    def ring(h, stage, step):
        along_x = (h == 0) == (stage == 1)
        return place(dx=step) if along_x else place(dy=step)

    counter = [0]

    def ag(h, s1, s2, to1, to2, device):
        ref = piece(h, s1, s2)
        remote(ref, ref, ag_send.at[counter[0] // 24], ag_recv.at[h, to1, to2], device)
        counter[0] += 1

    def ag_first(h):
        ag(h, 3, 3, 0, 3, ring(h, 1, d))
        ag(h, 3, 3, 1, 3, ring(h, 1, -d))

    def ag_second(h, s1):
        ag(h, s1, 3, s1, 0, ring(h, 2, d))
        ag(h, s1, 3, s1, 1, ring(h, 2, -d))

    def to_mate(h, s1, s2):
        ref = piece(h, s1, s2)
        late = (s2 if h == 0 else s1) == 2
        remote(ref, ref, mate_send, mate_recv.at[int(late)], mate)

    def ag_wait(h, s1, s2):
        arrived(piece(h, s1, s2), ag_recv.at[h, s1, s2])
        to_mate(h, s1, s2)

    own_piece = panel.at[x * 2 + k, z]
    pack_ref = packs.at[3]

    def phi_part(chunk):
        return pl.ds(chunk * 128, 128)

    def phi_first(chunk):
        for slot, way in ((0, d), (1, -d)):
            remote(
                phi_ref.at[phi_part(chunk)], phis.at[slot, phi_part(chunk)],
                phi_send, phi_recv.at[chunk] if slot == 0 else phi_rest.at[slot - 1], place(dz=way),
            )

    def phi_relay(chunk):
        ref = phis.at[0, phi_part(chunk)]
        arrived(ref, phi_recv.at[chunk])
        remote(ref, phis.at[2, phi_part(chunk)], phi_send, phi_rest.at[1], place(dz=d))

    def pack_first():
        remote(pack_ref, packs.at[0], pack_send, pack_recv.at[0], place(dz=d))
        remote(pack_ref, packs.at[1], pack_send, pack_recv.at[1], place(dz=-d))

    def pack_relay():
        arrived(packs.at[0], pack_recv.at[0])
        remote(packs.at[0], packs.at[2], pack_send, pack_recv.at[2], place(dz=d))
        arrived(packs.at[1], pack_recv.at[1])

    def z_part(half):
        return pl.ds(half * 128, 128)

    def z_first(half):
        for slot, way in ((0, d), (1, -d)):
            remote(
                c_ref.at[z_part(half)], slices.at[z, z_part(half)], z_send, z_recv.at[slot, half], place(dz=way)
            )

    def z_relay(half):
        ref = slices.at[batch_of(0), z_part(half)]
        arrived(ref, z_recv.at[0, half])
        remote(ref, ref, z_send, z_recv.at[2, half], place(dz=d))

    def z_wait(slot):
        for half in range(2):
            arrived(slices.at[batch_of(slot), z_part(half)], z_recv.at[slot, half])

    def pack_own():
        window_start = lax.rem(row + 31, 32) * 256
        index = list_ref[...] - window_start
        packs[3, 0:1, :] = jnp.where(index < 0, index + 8192, index).astype(f32)
        point = lax.broadcasted_iota(jnp.int32, (1, 512), 1)
        packs[3, 1:2, :] = jnp.where(point < count_ref[0], weight_ref[...], 0.0)

    def zero_fill():
        pot_ref[...] = jnp.zeros_like(pot_ref)

    def select(slot):
        if slot == 2:
            arrived(packs.at[2], pack_recv.at[2])
        index = packs[slot, 0:1, :]
        slots = lax.broadcasted_iota(jnp.int32, (768, 512), 0).astype(f32)
        selectors[slot] = jnp.where(slots == index, 1.0, 0.0).astype(bf16)

    def spread_batch(slot):
        ref = phi_ref if slot == 3 else phis.at[slot]
        spread[:, slot * 512 : slot * 512 + 512] = lax.dot_general(
            selectors[slot], ref[...], NT, preferred_element_type=f32
        ).astype(bf16)

    def batch_of(slot):
        return lax.rem(z + OFFSET[slot] * d + 8, 4)

    def partial_rho(slot):
        mixed = jnp.dot(
            window_t[...], spread[:, slot * 512 : slot * 512 + 512], preferred_element_type=f32
        )
        rho_own[batch_of(slot)] = 2.0 * jnp.sum(mixed * mixed, axis=0, keepdims=True)

    def turn_window(side):
        if side == 1:
            window_t[:, 256:512] = c_ref[...].T
        else:
            index = side // 2
            arrived(window.at[index], win_recv.at[index])
            window_t[:, side * 256 : side * 256 + 256] = window[index].T

    def spread_arrived(slot):
        arrived(phis.at[slot], phi_rest.at[slot - 1])
        spread_batch(slot)

    zero_fill()
    loads[0].wait()
    loads[1].wait()
    pack_own()
    select(3)
    loads[2].wait()
    spread_batch(3)
    loads[3].wait()
    turn_window(1)
    pl.semaphore_wait(barrier, len(friends) + 2 * off_diag.astype(jnp.int32))

    pltpu.make_async_copy(c_ref, slices.at[z], load_sem.at[0]).start()

    @pl.when(off_diag)
    def _():
        for h in range(2):
            part = pl.ds(h * 128, 128)
            remote(
                c_ref.at[part], own_piece.at[part], turn_send, ag_recv.at[h, 3, 3], turn_to, keep=False
            ).start()

    @pl.when(diag)
    def _():
        pltpu.make_async_copy(c_ref, own_piece, local_sem).start()

    pack_first()

    def window_first(far):
        for side, dr, edge in ((0, 1, 7), (1, -1, 0)):
            is_far = lax.rem(row, 8) == edge

            @pl.when(is_far if far else jnp.logical_not(is_far))
            def _():
                remote(c_ref, window.at[side], win_send, win_recv.at[side], shifted(dr, 0))

    def turn_wait(h):
        @pl.when(off_diag)
        def _():
            arrived(piece(h, 3, 3), ag_recv.at[h, 3, 3])

        if h == 0:

            @pl.when(diag)
            def _():
                pltpu.make_async_copy(c_ref, own_piece, local_sem).wait()

    def stage_one(h, s1):
        ag_wait(h, s1, 3)
        if s1 == 0:
            ag(h, 0, 3, 2, 3, ring(h, 1, d))

    def stage_two(h, s1, s2):
        ag_wait(h, s1, s2)
        if s2 == 0:
            ag(h, s1, 0, s1, 2, ring(h, 2, d))

    from_holder = lax.rem(z - y + 4, 4)

    def rho_out():
        @pl.when(off_diag)
        def _():
            remote(
                rho_own, rho_in.at[from_holder], rho_send, rho_recv.at[from_holder], holder, keep=False
            ).start()

    strips = (2 * k, 2 - 2 * k, 1)

    def block_place(strip, t):
        column = lax.rem(row + strip - 1 + 32, 32)
        line = lax.rem(row + t - 1 + 32, 32)
        return column, line

    def v_copy(strip, t, which=0):
        column, line = block_place(strip, t)
        return remote(
            v_out.at[strip, t], v_in.at[2 - strip, t], v_send.at[which], v_recv.at[2 - strip, t],
            (column, line // 8), keep=False,
        )

    def on_holder(call):
        return lambda *args: pl.when(diag)(functools.partial(call, *args))

    @on_holder
    def window_points():
        for o in (1, 2, 3):
            arrived(rho_in.at[o], rho_recv.at[o])
        for slot in range(4):
            b = batch_of(slot)
            rho = rho_own[b] + rho_in[1, b] + rho_in[2, b] + rho_in[3, b]
            pot = packs[slot, 1:2, :] * (-slater_coef * jnp.exp(jnp.log(rho + 1.0) * (1.0 / 3.0)))
            pots[:, slot * 512 : slot * 512 + 512] = pot

    def scale_rows(strip):
        rows = pl.ds(pl.multiple_of(strip * 256, 256), 256)
        scaled[rows, :] = (spread[rows, :].astype(f32) * pots[...]).astype(bf16)
        return scaled[rows, :]

    @on_holder
    def window_strip(order):
        strip = strips[order]
        columns = scale_rows(strip)
        halves = [
            lax.dot_general(spread[i * 384 : i * 384 + 384], columns, NT, preferred_element_type=f32)
            for i in range(2)
        ]
        side = jnp.concatenate(halves, axis=0)
        for t in range(3):
            v_out[strip, t] = side[t * 256 : t * 256 + 256].astype(bf16)
        for t in (strip, 1, 2 - strip):
            v_copy(strip, t).start()
        crossing[order] = side[256:512]
        if order == 0:
            _, line = block_place(1, strip)

            @pl.when(line // 8 != z)
            def _():
                v_out[1, strip] = crossing[0].T.astype(bf16)
                v_copy(1, strip, 1 + strip // 2).start()

    @on_holder
    def window_centre():
        centre = lax.dot_general(spread[256:512], scale_rows(1), NT, preferred_element_type=f32)
        for order, strip in ((2, 1), (0, strips[0]), (1, strips[1])):
            total = centre if order == 2 else crossing[order].T
            _, line = block_place(1, strip)
            rows = pl.ds(pl.multiple_of(lax.rem(line, 8) * 256, 256), 256)
            if order == 0:

                @pl.when(line // 8 == z)
                def _():
                    pot_ref[rows, :] += total

            else:
                pot_ref[rows, :] += total

    late_panel = lax.rem(2 * z - y + 6, 4)
    late_own = lax.rem(z + 2, 4)
    first_early = lax.rem(late_panel + 1 + (late_own == lax.rem(late_panel + 1, 4)).astype(jnp.int32), 4)
    second_early = lax.rem(late_panel + 3 - (late_own == lax.rem(late_panel + 3, 4)).astype(jnp.int32), 4)

    def add_slices(indices, last):
        def quad_step(quad, carry):
            for i in range(2):
                rows = pl.ds(pl.multiple_of((2 * quad + i) * 512, 512), 512)
                total = sum(
                    lax.dot_general(
                        panel[pl.ds(4 * quad + 2 * i, 2), b].reshape(512, 512), slices[b], NT,
                        preferred_element_type=f32,
                    )
                    for b in indices
                )
                if last:
                    dens_ref[rows, :] = (2.0 * (dens_sum[rows, :] + total)).astype(bf16)
                else:
                    dens_sum[rows, :] = total
            return carry

        lax.fori_loop(0, 2, quad_step, 0)

    def density_early():
        pltpu.make_async_copy(c_ref, slices.at[z], load_sem.at[0]).wait()
        arrived(panel.at[0:3], mate_recv.at[0])

        @pl.when(diag)
        def _():
            z_wait(1)
            add_slices([lax.rem(z + o, 4) for o in (0, 1, 3)], False)

        @pl.when(off_diag)
        def _():
            z_wait(1)
            add_slices([first_early, second_early], False)

    def density_late():
        z_wait(2)
        arrived(panel.at[0], mate_recv.at[1])

        @pl.when(diag)
        def _():
            add_slices([late_own], True)

        @pl.when(off_diag)
        def _():
            add_slices([late_panel, late_own], True)

    def left(ref, send_sem):
        pltpu.make_async_remote_copy(
            src_ref=ref, dst_ref=ref, send_sem=send_sem, recv_sem=mate_recv.at[0],
            device_id=mate, device_id_type=MESH,
        ).wait_send()

    def all_left():
        for ref, sem in (
            (panel.at[0:3], ag_send.at[0]), (panel.at[0, 0:3], ag_send.at[1]), (panel.at[0:4], mate_send),
            (slices.at[0:3], z_send), (phis, phi_send), (packs.at[0:3], pack_send), (window, win_send),
        ):
            left(ref, sem)

    steps = [
        (window_first, False), (phi_first, 0), (phi_first, 1), (phi_first, 2),
        (turn_wait, 0), (ag_first, 0), (phi_first, 3),
        (turn_wait, 1), (ag_first, 1), (ag_second, 0, 3), (ag_second, 1, 3),
        (to_mate, 0, 3, 3), (to_mate, 1, 3, 3), (pack_relay,), (select, 0), (select, 1),
        (stage_one, 0, 0), (window_first, True), (phi_relay, 0), (phi_relay, 1),
        (stage_one, 1, 0), (ag_second, 0, 0), (ag_second, 1, 0),
        (stage_one, 0, 1), (ag_second, 0, 1), (stage_one, 1, 1), (ag_second, 1, 1), (phi_relay, 2), (select, 2),
        (stage_two, 1, 3, 0), (stage_two, 0, 3, 0), (phi_relay, 3),
        (stage_one, 0, 2), (ag_second, 0, 2), (stage_one, 1, 2), (ag_second, 1, 2),
        (spread_batch, 0),
        (stage_two, 1, 0, 0), (stage_two, 0, 0, 0), (spread_arrived, 1), (z_first, 0),
        (turn_window, 0), (turn_window, 2), (partial_rho, 3), (partial_rho, 0),
        (stage_two, 1, 1, 0), (stage_two, 0, 1, 0), (partial_rho, 1),
        (spread_arrived, 2), (partial_rho, 2), (rho_out,), (z_first, 1), (z_relay, 0),
        (stage_two, 1, 2, 0), (stage_two, 0, 2, 0),
        (stage_two, 0, 3, 1), (stage_two, 1, 3, 1), (stage_two, 0, 0, 1), (stage_two, 1, 0, 1),
        (stage_two, 0, 3, 2), (stage_two, 1, 3, 2), (z_relay, 1), (stage_two, 0, 1, 1), (stage_two, 1, 1, 1),
        (window_points,), (window_strip, 0),
        (stage_two, 0, 2, 1), (stage_two, 1, 2, 1), (stage_two, 0, 0, 2), (stage_two, 1, 0, 2),
        (window_strip, 1),
        (stage_two, 1, 1, 2), (stage_two, 0, 1, 2), (stage_two, 0, 2, 2), (stage_two, 1, 2, 2),
        (density_early,), (window_centre,), (density_late,), (all_left,),
    ]
    for call, *args in steps:
        call(*args)

    for s in range(3):
        for t in range(3):
            source = lax.rem(row + s - 1 + 32, 32)
            line = lax.rem(source + t - 1 + 32, 32)
            coming = line // 8 == z
            if s == 1:
                coming = jnp.logical_and(coming, source // 8 != z)

            @pl.when(coming)
            def _():
                arrived(v_in.at[s, t], v_recv.at[s, t])
                pot_ref[pl.ds(pl.multiple_of(lax.rem(line, 8) * 256, 256), 256), :] += v_in[s, t].astype(f32)

    @pl.when(off_diag)
    def _():
        left(own_piece, turn_send)
        left(rho_own, rho_send)

    @pl.when(diag)
    def _():
        left(v_out.at[0:2], v_send.at[0])
        for t in (0, 2):
            _, line = block_place(1, t)

            @pl.when(line // 8 != z)
            def _():
                left(v_out.at[1, t], v_send.at[1 + t // 2])


def on_device(coeffs, basis_values, point_weights, point_counts, func_lists):
    dma = pltpu.SemaphoreType.DMA
    density, potential = pl.pallas_call(
        kernel,
        out_shape=(
            pltpu.VMEM((2048, 256), bf16),
            pltpu.VMEM((2048, 256), f32),
        ),
        in_specs=[pl.BlockSpec(memory_space=pltpu.SMEM)] + [pl.BlockSpec(memory_space=pltpu.HBM)] * 4,
        out_specs=(pl.BlockSpec(memory_space=pltpu.VMEM),) * 2,
        scratch_shapes=[
            pltpu.VMEM((256, 512), bf16),
            pltpu.VMEM((512, 512), bf16),
            pltpu.VMEM((1, 512), jnp.int32),
            pltpu.VMEM((1, 512), f32),
            pltpu.VMEM((8, 4, 256, 512), bf16),
            pltpu.VMEM((4, 256, 512), bf16),
            pltpu.VMEM((2, 256, 512), bf16),
            pltpu.VMEM((3, 512, 512), bf16),
            pltpu.VMEM((4, 8, 512), f32),
            pltpu.VMEM((512, 768), bf16),
            pltpu.VMEM((4, 768, 512), bf16),
            pltpu.VMEM((768, 2048), bf16),
            pltpu.VMEM((768, 2048), bf16),
            pltpu.VMEM((4, 1, 512), f32),
            pltpu.VMEM((4, 4, 1, 512), f32),
            pltpu.VMEM((2, 256, 256), f32),
            pltpu.VMEM((1, 2048), f32),
            pltpu.VMEM((2048, 256), f32),
            pltpu.VMEM((3, 3, 256, 256), bf16),
            pltpu.VMEM((3, 3, 256, 256), bf16),
            dma((2,)), dma((2, 4, 4)), dma, dma((2,)),
            dma, dma((3, 2)), dma, dma((4,)), dma((2,)), dma, dma((3,)),
            dma, dma, dma((2,)), dma, dma((4,)), dma((3,)), dma((3, 3)), dma, dma((4,)),
        ],
        compiler_params=pltpu.CompilerParams(
            collective_id=0, has_side_effects=True, vmem_limit_bytes=36 * 1024 * 1024
        ),
    )(
        point_counts,
        *(
            pltpu.with_memory_space_constraint(array, pltpu.HBM)
            for array in (coeffs, basis_values.reshape(512, 512), func_lists, point_weights)
        ),
    )
    return density, potential


def solution(mesh):
    in_specs = (
        P("row", "col"),
        P(("row", "col"), None, None),
        P(("row", "col"), None),
        P(("row", "col")),
        P(("row", "col"), None),
    )
    out_specs = (P("col", "row"), P("col", "row"))
    return jax.shard_map(
        on_device, mesh=mesh, in_specs=in_specs, out_specs=out_specs, check_vma=False
    )
```

```python
import functools
import jax
import jax.numpy as jnp
from jax import lax
from jax.experimental import pallas as pl
from jax.experimental.pallas import tpu as pltpu
from jax.sharding import PartitionSpec as P

slater_coef = 0.9847450218426965
MESH = pl.DeviceIdType.MESH
f32 = jnp.float32
bf16 = jnp.bfloat16

OFFSET = (-1, 1, 2, 0)
ROWS = ((0, 112), (112, 144))
NT = (((1,), (1,)), ((), ()))


def kernel(
    count_ref, c_hbm, phi_hbm, list_hbm, weight_hbm, dens_ref, pot_ref,
    c_ref, phi_ref, list_ref, weight_ref,
    panel, slices, window, phis, packs, window_t, selectors, spread, scaled, rho_own, rho_in, crossing, pots, dens_sum, v_out, v_in,
    ag_send, ag_recv, mate_send, mate_recv, z_send, z_behind, z_ahead, z_recv, phi_send, phi_recv, phi_rest, pack_send, pack_recv,
    turn_send, win_send, win_recv, rho_send, rho_recv, v_send, v_recv, local_sem, load_sem,
):
    row = lax.axis_index("row")
    z = lax.axis_index("col")
    k = lax.rem(row, 2)
    x = lax.rem(row // 2, 4)
    y = row // 8
    d = 1 - 2 * k
    diag = y == z
    off_diag = y != z

    def place(dx=0, dy=0, dz=0, core=None):
        xx = lax.rem(x + dx + 8, 4)
        yy = lax.rem(y + dy + 8, 4)
        core = k if core is None else core
        return ((yy * 4 + xx) * 2 + core, lax.rem(z + dz + 8, 4))

    def shifted(dr, dz):
        return (lax.rem(row + dr + 32, 32), lax.rem(z + dz + 4, 4))

    mate = place(core=1 - k)
    turn_to = ((lax.rem(2 * y - z + 8, 4) * 4 + x) * 2 + k, y)
    turn_from = ((z * 4 + x) * 2 + k, lax.rem(2 * z - y + 8, 4))
    holder = (row, y)

    loads = [
        pltpu.make_async_copy(source, target, load_sem.at[i])
        for i, (source, target) in enumerate(
            ((list_hbm, list_ref), (weight_hbm, weight_ref), (phi_hbm, phi_ref), (c_hbm, c_ref))
        )
    ]
    for load in loads:
        load.start()
    barrier = pltpu.get_barrier_semaphore()
    friends = [mate, place(dx=1), place(dx=-1), place(dy=1), place(dy=-1), place(dz=2)]
    friends += [shifted(dr, dz) for dr in (-1, 0, 1) for dz in (-1, 0, 1) if dr or dz]
    for friend in friends:
        pl.semaphore_signal(barrier, inc=1, device_id=friend, device_id_type=MESH)

    @pl.when(off_diag)
    def _():
        for friend in (turn_to, turn_from):
            pl.semaphore_signal(barrier, inc=1, device_id=friend, device_id_type=MESH)

    def remote(src, dst, send_sem, recv_sem, device, keep=True):
        copy = pltpu.make_async_remote_copy(
            src_ref=src, dst_ref=dst, send_sem=send_sem, recv_sem=recv_sem,
            device_id=device, device_id_type=MESH,
        )
        if keep:
            copy.start()
        return copy

    def arrived(dst, recv_sem):
        pltpu.make_async_remote_copy(
            src_ref=dst, dst_ref=dst, send_sem=mate_send, recv_sem=recv_sem,
            device_id=mate, device_id_type=MESH,
        ).wait_recv()

    def part(h):
        return pl.ds(ROWS[h][0], ROWS[h][1])

    def piece(h, s1, s2, core=None):
        core_now, way = (k, d) if core is None else (1 - k, -d)
        first, second = (x, y) if h == 0 else (y, x)
        o1 = lax.rem(first + OFFSET[s1] * way + 8, 4)
        o2 = lax.rem(second + OFFSET[s2] * way + 8, 4)
        sx, sy = (o1, o2) if h == 0 else (o2, o1)
        return panel.at[sx * 2 + core_now, lax.rem(2 * z - sy + 8, 4), part(h)]

    def ring(h, stage, step):
        along_x = (h == 0) == (stage == 1)
        return place(dx=step) if along_x else place(dy=step)

    def ag(h, s1, s2, to1, to2, device):
        ref = piece(h, s1, s2)
        remote(ref, ref, ag_send.at[h], ag_recv.at[h, to1, to2], device)

    def ag_first(h):
        ag(h, 3, 3, 0, 3, ring(h, 1, d))
        ag(h, 3, 3, 1, 3, ring(h, 1, -d))

    def ag_second(h, s1):
        ag(h, s1, 3, s1, 0, ring(h, 2, d))
        ag(h, s1, 3, s1, 1, ring(h, 2, -d))

    def to_mate(h, s1, s2):
        ref = piece(h, s1, s2)
        late = (s2 if h == 0 else s1) == 2
        remote(ref, ref, mate_send, mate_recv.at[int(late)], mate)

    def ag_wait(h, s1, s2):
        arrived(piece(h, s1, s2), ag_recv.at[h, s1, s2])
        to_mate(h, s1, s2)

    own_piece = panel.at[x * 2 + k, z]
    pack_ref = packs.at[3]

    def phi_part(chunk):
        return pl.ds(chunk * 128, 128)

    def phi_first(chunk):
        for slot, way in ((0, d), (1, -d)):
            remote(
                phi_ref.at[phi_part(chunk)], phis.at[slot, phi_part(chunk)],
                phi_send, phi_recv.at[chunk] if slot == 0 else phi_rest.at[slot - 1], place(dz=way),
            )

    def phi_relay(chunk):
        ref = phis.at[0, phi_part(chunk)]
        arrived(ref, phi_recv.at[chunk])
        remote(ref, phis.at[2, phi_part(chunk)], phi_send, phi_rest.at[1], place(dz=d))

    def pack_first():
        remote(pack_ref, packs.at[0], pack_send, pack_recv.at[0], place(dz=d))
        remote(pack_ref, packs.at[1], pack_send, pack_recv.at[1], place(dz=-d))

    def pack_relay():
        arrived(packs.at[0], pack_recv.at[0])
        remote(packs.at[0], packs.at[2], pack_send, pack_recv.at[2], place(dz=d))
        arrived(packs.at[1], pack_recv.at[1])

    def z_part(half):
        return pl.ds(half * 128, 128)

    def z_first(half):
        remote(c_ref.at[z_part(half)], slices.at[z, z_part(half)], z_send, z_recv.at[0, half], place(dz=d))

        @pl.when(lax.rem(z - d + 4, 4) != y)
        def _():
            remote(
                c_ref.at[z_part(half)], slices.at[z, z_part(half)], z_behind, z_recv.at[1, half], place(dz=-d)
            )

    def z_relay(half):
        ref = slices.at[batch_of(0), z_part(half)]
        arrived(ref, z_recv.at[0, half])

        @pl.when(lax.rem(z + d + 4, 4) != y)
        def _():
            remote(ref, ref, z_ahead, z_recv.at[2, half], place(dz=d))

    def z_wait(slot):
        for half in range(2):
            arrived(slices.at[batch_of(slot), z_part(half)], z_recv.at[slot, half])

    def pack_own():
        window_start = lax.rem(row + 31, 32) * 256
        index = list_ref[...] - window_start
        packs[3, 0:1, :] = jnp.where(index < 0, index + 8192, index).astype(f32)
        point = lax.broadcasted_iota(jnp.int32, (1, 512), 1)
        packs[3, 1:2, :] = jnp.where(point < count_ref[0], weight_ref[...], 0.0)

    def zero_fill():
        pot_ref[...] = jnp.zeros_like(pot_ref)

    def select(slot):
        if slot == 2:
            arrived(packs.at[2], pack_recv.at[2])
        index = packs[slot, 0:1, :]
        slots = lax.broadcasted_iota(jnp.int32, (768, 512), 0).astype(f32)
        selectors[slot] = jnp.where(slots == index, 1.0, 0.0).astype(bf16)

    def spread_batch(slot):
        ref = phi_ref if slot == 3 else phis.at[slot]
        spread[:, slot * 512 : slot * 512 + 512] = lax.dot_general(
            selectors[slot], ref[...], NT, preferred_element_type=f32
        ).astype(bf16)

    def batch_of(slot):
        return lax.rem(z + OFFSET[slot] * d + 8, 4)

    def partial_rho(slot):
        mixed = jnp.dot(
            window_t[...], spread[:, slot * 512 : slot * 512 + 512], preferred_element_type=f32
        )
        rho_own[batch_of(slot)] = 2.0 * jnp.sum(mixed * mixed, axis=0, keepdims=True)

    def turn_window(side):
        if side == 1:
            window_t[:, 256:512] = c_ref[...].T
        else:
            index = side // 2
            arrived(window.at[index], win_recv.at[index])
            window_t[:, side * 256 : side * 256 + 256] = window[index].T

    def spread_arrived(slot):
        arrived(phis.at[slot], phi_rest.at[slot - 1])
        spread_batch(slot)

    zero_fill()
    loads[0].wait()
    loads[1].wait()
    pack_own()
    select(3)
    loads[2].wait()
    spread_batch(3)
    loads[3].wait()
    turn_window(1)
    pl.semaphore_wait(barrier, len(friends) + 2 * off_diag.astype(jnp.int32))

    pltpu.make_async_copy(c_ref, slices.at[z], load_sem.at[0]).start()

    @pl.when(off_diag)
    def _():
        for h in range(2):
            remote(
                c_ref.at[part(h)], own_piece.at[part(h)], turn_send, ag_recv.at[h, 3, 3], turn_to, keep=False
            ).start()

    @pl.when(diag)
    def _():
        pltpu.make_async_copy(c_ref, own_piece, local_sem).start()

    pack_first()

    def window_first(far):
        for side, dr, edge in ((0, 1, 7), (1, -1, 0)):
            is_far = lax.rem(row, 8) == edge

            @pl.when(is_far if far else jnp.logical_not(is_far))
            def _():
                remote(c_ref, window.at[side], win_send, win_recv.at[side], shifted(dr, 0))

    def turn_wait(h):
        @pl.when(off_diag)
        def _():
            arrived(piece(h, 3, 3), ag_recv.at[h, 3, 3])

        if h == 0:

            @pl.when(diag)
            def _():
                pltpu.make_async_copy(c_ref, own_piece, local_sem).wait()

    def stage_one(h, s1):
        ag_wait(h, s1, 3)
        if s1 == 0:
            ag(h, 0, 3, 2, 3, ring(h, 1, d))

    def stage_two(h, s1, s2):
        ag_wait(h, s1, s2)
        if s2 == 0:
            ag(h, s1, 0, s1, 2, ring(h, 2, d))

    from_holder = lax.rem(z - y + 4, 4)

    def rho_out():
        @pl.when(off_diag)
        def _():
            remote(
                rho_own, rho_in.at[from_holder], rho_send, rho_recv.at[from_holder], holder, keep=False
            ).start()

    strips = (2 * k, 2 - 2 * k, 1)

    def block_place(strip, t):
        column = lax.rem(row + strip - 1 + 32, 32)
        line = lax.rem(row + t - 1 + 32, 32)
        return column, line

    def v_copy(strip, t, which=0):
        column, line = block_place(strip, t)
        return remote(
            v_out.at[strip, t], v_in.at[2 - strip, t], v_send.at[which], v_recv.at[2 - strip, t],
            (column, line // 8), keep=False,
        )

    def on_holder(call):
        return lambda *args: pl.when(diag)(functools.partial(call, *args))

    @on_holder
    def window_points():
        for o in (1, 2, 3):
            arrived(rho_in.at[o], rho_recv.at[o])
        for slot in range(4):
            b = batch_of(slot)
            rho = rho_own[b] + rho_in[1, b] + rho_in[2, b] + rho_in[3, b]
            pot = packs[slot, 1:2, :] * (-slater_coef * jnp.exp(jnp.log(rho + 1.0) * (1.0 / 3.0)))
            pots[:, slot * 512 : slot * 512 + 512] = pot

    def scale_rows(strip):
        rows = pl.ds(pl.multiple_of(strip * 256, 256), 256)
        scaled[rows, :] = (spread[rows, :].astype(f32) * pots[...]).astype(bf16)
        return scaled[rows, :]

    @on_holder
    def window_strip(order):
        strip = strips[order]
        columns = scale_rows(strip)
        halves = [
            lax.dot_general(spread[i * 384 : i * 384 + 384], columns, NT, preferred_element_type=f32)
            for i in range(2)
        ]
        side = jnp.concatenate(halves, axis=0)
        for t in range(3):
            v_out[strip, t] = side[t * 256 : t * 256 + 256].astype(bf16)
        for t in (strip, 1, 2 - strip):
            v_copy(strip, t).start()
        crossing[order] = side[256:512]
        if order == 0:
            _, line = block_place(1, strip)

            @pl.when(line // 8 != z)
            def _():
                v_out[1, strip] = crossing[0].T.astype(bf16)
                v_copy(1, strip, 1 + strip // 2).start()

    @on_holder
    def window_centre():
        centre = lax.dot_general(spread[256:512], scale_rows(1), NT, preferred_element_type=f32)
        for order, strip in ((2, 1), (0, strips[0]), (1, strips[1])):
            total = centre if order == 2 else crossing[order].T
            _, line = block_place(1, strip)
            rows = pl.ds(pl.multiple_of(lax.rem(line, 8) * 256, 256), 256)
            if order == 0:

                @pl.when(line // 8 == z)
                def _():
                    pot_ref[rows, :] += total

            else:
                pot_ref[rows, :] += total

    late_panel = lax.rem(2 * z - y + 6, 4)
    late_own = lax.rem(z + 2, 4)
    first_early = lax.rem(late_panel + 1 + (late_own == lax.rem(late_panel + 1, 4)).astype(jnp.int32), 4)
    second_early = lax.rem(late_panel + 3 - (late_own == lax.rem(late_panel + 3, 4)).astype(jnp.int32), 4)

    def add_slices(indices, last, rows_of=lambda b: slices[b]):
        def quad_step(quad, carry):
            for i in range(2):
                rows = pl.ds(pl.multiple_of((2 * quad + i) * 512, 512), 512)
                total = sum(
                    lax.dot_general(
                        panel[pl.ds(4 * quad + 2 * i, 2), b].reshape(512, 512), rows_of(b), NT,
                        preferred_element_type=f32,
                    )
                    for b in indices
                )
                if last:
                    dens_ref[rows, :] = (2.0 * (dens_sum[rows, :] + total)).astype(bf16)
                else:
                    dens_sum[rows, :] = total
            return carry

        lax.fori_loop(0, 2, quad_step, 0)

    def density_early():
        pltpu.make_async_copy(c_ref, slices.at[z], load_sem.at[0]).wait()
        arrived(panel.at[0:3], mate_recv.at[0])

        @pl.when(diag)
        def _():
            add_slices([lax.rem(z + o, 4) for o in (0, 1, 3)], False, own_rows)

        @pl.when(off_diag)
        def _():
            z_wait(1)
            add_slices([first_early, second_early], False)

    def own_rows(b):
        return panel[x * 2 + k, b]

    def density_late():
        arrived(panel.at[0], mate_recv.at[1])

        @pl.when(diag)
        def _():
            add_slices([late_own], True, own_rows)

        @pl.when(off_diag)
        def _():
            z_wait(2)
            add_slices([late_panel, late_own], True)

    def left(ref, send_sem):
        pltpu.make_async_remote_copy(
            src_ref=ref, dst_ref=ref, send_sem=send_sem, recv_sem=mate_recv.at[0],
            device_id=mate, device_id_type=MESH,
        ).wait_send()

    def all_left():
        for ref, sem in (
            (panel.at[0:5, 0:3, part(0)], ag_send.at[0]), (panel.at[0:5, 0:3, part(1)], ag_send.at[1]),
            (panel.at[0:4], mate_send),
            (slices.at[0], z_send), (phis, phi_send), (packs.at[0:3], pack_send), (window, win_send),
        ):
            left(ref, sem)
        pl.when(lax.rem(z - d + 4, 4) != y)(lambda: left(slices.at[0], z_behind))
        pl.when(lax.rem(z + d + 4, 4) != y)(lambda: left(slices.at[0], z_ahead))

    steps = [
        (window_first, False), (phi_first, 0), (phi_first, 1), (phi_first, 2),
        (turn_wait, 0), (ag_first, 0), (phi_first, 3),
        (turn_wait, 1), (ag_first, 1), (ag_second, 0, 3), (ag_second, 1, 3),
        (to_mate, 0, 3, 3), (to_mate, 1, 3, 3), (pack_relay,), (select, 0), (select, 1),
        (stage_one, 0, 0), (window_first, True), (phi_relay, 0), (phi_relay, 1),
        (stage_one, 1, 0), (ag_second, 0, 0), (ag_second, 1, 0),
        (stage_one, 0, 1), (ag_second, 0, 1), (stage_one, 1, 1), (ag_second, 1, 1), (phi_relay, 2), (select, 2),
        (stage_two, 1, 3, 0), (stage_two, 0, 3, 0), (phi_relay, 3), (spread_batch, 0),
        (stage_one, 0, 2), (ag_second, 0, 2), (turn_window, 0), (turn_window, 2), (partial_rho, 3),
        (stage_one, 1, 2), (ag_second, 1, 2), (partial_rho, 0), (spread_arrived, 1), (z_first, 0), (partial_rho, 1),
        (stage_two, 1, 0, 0), (stage_two, 0, 0, 0), (stage_two, 1, 1, 0), (stage_two, 0, 1, 0),
        (spread_arrived, 2), (partial_rho, 2), (rho_out,), (z_first, 1), (z_relay, 0),
        (stage_two, 1, 2, 0), (stage_two, 0, 2, 0),
        (stage_two, 0, 3, 1), (stage_two, 1, 3, 1), (stage_two, 0, 0, 1), (stage_two, 1, 0, 1),
        (stage_two, 0, 3, 2), (stage_two, 1, 3, 2), (stage_two, 0, 1, 1), (stage_two, 1, 1, 1),
        (window_points,), (window_strip, 0), (z_relay, 1),
        (stage_two, 0, 2, 1), (stage_two, 1, 2, 1), (stage_two, 0, 0, 2), (stage_two, 1, 0, 2),
        (window_strip, 1),
        (stage_two, 1, 1, 2), (stage_two, 0, 1, 2), (stage_two, 0, 2, 2), (stage_two, 1, 2, 2),
        (density_early,), (window_centre,), (density_late,), (all_left,),
    ]
    for call, *args in steps:
        call(*args)

    for s in range(3):
        for t in range(3):
            source = lax.rem(row + s - 1 + 32, 32)
            line = lax.rem(source + t - 1 + 32, 32)
            coming = line // 8 == z
            if s == 1:
                coming = jnp.logical_and(coming, source // 8 != z)

            @pl.when(coming)
            def _():
                arrived(v_in.at[s, t], v_recv.at[s, t])
                pot_ref[pl.ds(pl.multiple_of(lax.rem(line, 8) * 256, 256), 256), :] += v_in[s, t].astype(f32)

    @pl.when(off_diag)
    def _():
        left(own_piece, turn_send)
        left(rho_own, rho_send)

    @pl.when(diag)
    def _():
        left(v_out.at[0:2], v_send.at[0])
        for t in (0, 2):
            _, line = block_place(1, t)

            @pl.when(line // 8 != z)
            def _():
                left(v_out.at[1, t], v_send.at[1 + t // 2])


def on_device(coeffs, basis_values, point_weights, point_counts, func_lists):
    dma = pltpu.SemaphoreType.DMA
    density, potential = pl.pallas_call(
        kernel,
        out_shape=(
            pltpu.VMEM((2048, 256), bf16),
            pltpu.VMEM((2048, 256), f32),
        ),
        in_specs=[pl.BlockSpec(memory_space=pltpu.SMEM)] + [pl.BlockSpec(memory_space=pltpu.HBM)] * 4,
        out_specs=(pl.BlockSpec(memory_space=pltpu.VMEM),) * 2,
        scratch_shapes=[
            pltpu.VMEM((256, 512), bf16),
            pltpu.VMEM((512, 512), bf16),
            pltpu.VMEM((1, 512), jnp.int32),
            pltpu.VMEM((1, 512), f32),
            pltpu.VMEM((8, 4, 256, 512), bf16),
            pltpu.VMEM((4, 256, 512), bf16),
            pltpu.VMEM((2, 256, 512), bf16),
            pltpu.VMEM((3, 512, 512), bf16),
            pltpu.VMEM((4, 8, 512), f32),
            pltpu.VMEM((512, 768), bf16),
            pltpu.VMEM((4, 768, 512), bf16),
            pltpu.VMEM((768, 2048), bf16),
            pltpu.VMEM((768, 2048), bf16),
            pltpu.VMEM((4, 1, 512), f32),
            pltpu.VMEM((4, 4, 1, 512), f32),
            pltpu.VMEM((2, 256, 256), f32),
            pltpu.VMEM((1, 2048), f32),
            pltpu.VMEM((2048, 256), f32),
            pltpu.VMEM((3, 3, 256, 256), bf16),
            pltpu.VMEM((3, 3, 256, 256), bf16),
            dma((2,)), dma((2, 4, 4)), dma, dma((2,)),
            dma, dma, dma, dma((3, 2)), dma, dma((4,)), dma((2,)), dma, dma((3,)),
            dma, dma, dma((2,)), dma, dma((4,)), dma((3,)), dma((3, 3)), dma, dma((4,)),
        ],
        compiler_params=pltpu.CompilerParams(
            collective_id=0, has_side_effects=True, vmem_limit_bytes=36 * 1024 * 1024
        ),
    )(
        point_counts,
        *(
            pltpu.with_memory_space_constraint(array, pltpu.HBM)
            for array in (coeffs, basis_values.reshape(512, 512), func_lists, point_weights)
        ),
    )
    return density, potential


def solution(mesh):
    in_specs = (
        P("row", "col"),
        P(("row", "col"), None, None),
        P(("row", "col"), None),
        P(("row", "col")),
        P(("row", "col"), None),
    )
    out_specs = (P("col", "row"), P("col", "row"))
    return jax.shard_map(
        on_device, mesh=mesh, in_specs=in_specs, out_specs=out_specs, check_vma=False
    )
```

```python
import functools
import jax
import jax.numpy as jnp
from jax import lax
from jax.experimental import pallas as pl
from jax.experimental.pallas import tpu as pltpu
from jax.sharding import PartitionSpec as P

slater_coef = 0.9847450218426965
MESH = pl.DeviceIdType.MESH
f32 = jnp.float32
bf16 = jnp.bfloat16

OFFSET = (-1, 1, 2, 0)
ROWS = ((0, 112), (112, 144))
NT = (((1,), (1,)), ((), ()))


def kernel(
    count_ref, c_hbm, phi_hbm, list_hbm, weight_hbm, dens_ref, pot_ref,
    c_ref, phi_ref, list_ref, weight_ref,
    panel, slices, window, phis, packs, window_t, selectors, spread, scaled, rho_own, rho_in, crossing, pots, dens_sum, v_out, v_in,
    ag_send, ag_recv, mate_send, mate_recv, z_send, z_behind, z_ahead, z_recv, phi_send, phi_recv, phi_rest, pack_send, pack_recv,
    turn_send, win_send, win_recv, rho_send, rho_recv, v_send, v_recv, local_sem, load_sem,
):
    row = lax.axis_index("row")
    z = lax.axis_index("col")
    k = lax.rem(row, 2)
    x = lax.rem(row // 2, 4)
    y = row // 8
    d = 1 - 2 * k
    diag = y == z
    off_diag = y != z

    def place(dx=0, dy=0, dz=0, core=None):
        xx = lax.rem(x + dx + 8, 4)
        yy = lax.rem(y + dy + 8, 4)
        core = k if core is None else core
        return ((yy * 4 + xx) * 2 + core, lax.rem(z + dz + 8, 4))

    def shifted(dr, dz):
        return (lax.rem(row + dr + 32, 32), lax.rem(z + dz + 4, 4))

    mate = place(core=1 - k)
    turn_to = ((lax.rem(2 * y - z + 8, 4) * 4 + x) * 2 + k, y)
    turn_from = ((z * 4 + x) * 2 + k, lax.rem(2 * z - y + 8, 4))
    holder = (row, y)

    loads = [
        pltpu.make_async_copy(source, target, load_sem.at[i])
        for i, (source, target) in enumerate(
            ((list_hbm, list_ref), (weight_hbm, weight_ref), (phi_hbm, phi_ref), (c_hbm, c_ref))
        )
    ]
    for load in loads:
        load.start()
    barrier = pltpu.get_barrier_semaphore()
    friends = [mate, place(dx=1), place(dx=-1), place(dy=1), place(dy=-1), place(dz=2)]
    friends += [shifted(dr, dz) for dr in (-1, 0, 1) for dz in (-1, 0, 1) if dr or dz]
    for friend in friends:
        pl.semaphore_signal(barrier, inc=1, device_id=friend, device_id_type=MESH)

    @pl.when(off_diag)
    def _():
        for friend in (turn_to, turn_from):
            pl.semaphore_signal(barrier, inc=1, device_id=friend, device_id_type=MESH)

    def remote(src, dst, send_sem, recv_sem, device, keep=True):
        copy = pltpu.make_async_remote_copy(
            src_ref=src, dst_ref=dst, send_sem=send_sem, recv_sem=recv_sem,
            device_id=device, device_id_type=MESH,
        )
        if keep:
            copy.start()
        return copy

    def arrived(dst, recv_sem):
        pltpu.make_async_remote_copy(
            src_ref=dst, dst_ref=dst, send_sem=mate_send, recv_sem=recv_sem,
            device_id=mate, device_id_type=MESH,
        ).wait_recv()

    def part(h):
        return pl.ds(ROWS[h][0], ROWS[h][1])

    def piece(h, s1, s2, core=None):
        core_now, way = (k, d) if core is None else (1 - k, -d)
        first, second = (x, y) if h == 0 else (y, x)
        o1 = lax.rem(first + OFFSET[s1] * way + 8, 4)
        o2 = lax.rem(second + OFFSET[s2] * way + 8, 4)
        sx, sy = (o1, o2) if h == 0 else (o2, o1)
        return panel.at[sx * 2 + core_now, lax.rem(2 * z - sy + 8, 4), part(h)]

    def ring(h, stage, step):
        along_x = (h == 0) == (stage == 1)
        return place(dx=step) if along_x else place(dy=step)

    def ag(h, s1, s2, to1, to2, device):
        ref = piece(h, s1, s2)
        remote(ref, ref, ag_send.at[h], ag_recv.at[h, to1, to2], device)

    def ag_first(h):
        ag(h, 3, 3, 0, 3, ring(h, 1, d))
        ag(h, 3, 3, 1, 3, ring(h, 1, -d))

    def ag_second(h, s1):
        ag(h, s1, 3, s1, 0, ring(h, 2, d))
        ag(h, s1, 3, s1, 1, ring(h, 2, -d))

    def to_mate(h, s1, s2):
        ref = piece(h, s1, s2)
        late = (s2 if h == 0 else s1) == 2
        remote(ref, ref, mate_send, mate_recv.at[int(late)], mate)

    def ag_wait(h, s1, s2):
        arrived(piece(h, s1, s2), ag_recv.at[h, s1, s2])
        to_mate(h, s1, s2)

    own_piece = panel.at[x * 2 + k, z]
    pack_ref = packs.at[3]

    def phi_part(chunk):
        return pl.ds(chunk * 128, 128)

    def phi_first(chunk):
        for slot, way in ((0, d), (1, -d)):
            remote(
                phi_ref.at[phi_part(chunk)], phis.at[slot, phi_part(chunk)],
                phi_send, phi_recv.at[chunk] if slot == 0 else phi_rest.at[slot - 1], place(dz=way),
            )

    def phi_relay(chunk):
        ref = phis.at[0, phi_part(chunk)]
        arrived(ref, phi_recv.at[chunk])
        remote(ref, phis.at[2, phi_part(chunk)], phi_send, phi_rest.at[1], place(dz=d))

    def pack_first():
        remote(pack_ref, packs.at[0], pack_send, pack_recv.at[0], place(dz=d))
        remote(pack_ref, packs.at[1], pack_send, pack_recv.at[1], place(dz=-d))

    def pack_relay():
        arrived(packs.at[0], pack_recv.at[0])
        remote(packs.at[0], packs.at[2], pack_send, pack_recv.at[2], place(dz=d))
        arrived(packs.at[1], pack_recv.at[1])

    def z_part(half):
        return pl.ds(half * 128, 128)

    def z_first(half):
        remote(c_ref.at[z_part(half)], slices.at[z, z_part(half)], z_send, z_recv.at[0, half], place(dz=d))

        @pl.when(lax.rem(z - d + 4, 4) != y)
        def _():
            remote(
                c_ref.at[z_part(half)], slices.at[z, z_part(half)], z_behind, z_recv.at[1, half], place(dz=-d)
            )

    def z_relay(half):
        ref = slices.at[batch_of(0), z_part(half)]
        arrived(ref, z_recv.at[0, half])

        @pl.when(lax.rem(z + d + 4, 4) != y)
        def _():
            remote(ref, ref, z_ahead, z_recv.at[2, half], place(dz=d))

    def z_wait(slot):
        for half in range(2):
            arrived(slices.at[batch_of(slot), z_part(half)], z_recv.at[slot, half])

    def pack_own():
        window_start = lax.rem(row + 31, 32) * 256
        index = list_ref[...] - window_start
        packs[3, 0:1, :] = jnp.where(index < 0, index + 8192, index).astype(f32)
        point = lax.broadcasted_iota(jnp.int32, (1, 512), 1)
        packs[3, 1:2, :] = jnp.where(point < count_ref[0], weight_ref[...], 0.0)

    def zero_fill():
        pot_ref[...] = jnp.zeros_like(pot_ref)

    def select(slot):
        if slot == 2:
            arrived(packs.at[2], pack_recv.at[2])
        index = packs[slot, 0:1, :]
        slots = lax.broadcasted_iota(jnp.int32, (768, 512), 0).astype(f32)
        selectors[slot] = jnp.where(slots == index, 1.0, 0.0).astype(bf16)

    def spread_batch(slot):
        ref = phi_ref if slot == 3 else phis.at[slot]
        spread[:, slot * 512 : slot * 512 + 512] = lax.dot_general(
            selectors[slot], ref[...], NT, preferred_element_type=f32
        ).astype(bf16)

    def batch_of(slot):
        return lax.rem(z + OFFSET[slot] * d + 8, 4)

    def partial_rho(slot):
        mixed = jnp.dot(
            window_t[...], spread[:, slot * 512 : slot * 512 + 512], preferred_element_type=f32
        )
        rho_own[batch_of(slot)] = 2.0 * jnp.sum(mixed * mixed, axis=0, keepdims=True)

    def turn_window(side):
        if side == 1:
            window_t[:, 256:512] = c_ref[...].T
        else:
            index = side // 2
            arrived(window.at[index], win_recv.at[index])
            window_t[:, side * 256 : side * 256 + 256] = window[index].T

    def spread_arrived(slot):
        arrived(phis.at[slot], phi_rest.at[slot - 1])
        spread_batch(slot)

    zero_fill()
    loads[0].wait()
    loads[1].wait()
    pack_own()
    select(3)
    loads[2].wait()
    spread_batch(3)
    loads[3].wait()
    turn_window(1)
    pl.semaphore_wait(barrier, len(friends) + 2 * off_diag.astype(jnp.int32))

    pltpu.make_async_copy(c_ref, slices.at[z], load_sem.at[0]).start()

    @pl.when(off_diag)
    def _():
        for h in range(2):
            remote(
                c_ref.at[part(h)], own_piece.at[part(h)], turn_send, ag_recv.at[h, 3, 3], turn_to, keep=False
            ).start()

    @pl.when(diag)
    def _():
        pltpu.make_async_copy(c_ref, own_piece, local_sem).start()

    pack_first()

    def window_first(far):
        for side, dr, edge in ((0, 1, 7), (1, -1, 0)):
            is_far = lax.rem(row, 8) == edge

            @pl.when(is_far if far else jnp.logical_not(is_far))
            def _():
                remote(c_ref, window.at[side], win_send, win_recv.at[side], shifted(dr, 0))

    def turn_wait(h):
        @pl.when(off_diag)
        def _():
            arrived(piece(h, 3, 3), ag_recv.at[h, 3, 3])

        if h == 0:

            @pl.when(diag)
            def _():
                pltpu.make_async_copy(c_ref, own_piece, local_sem).wait()

    def stage_one(h, s1):
        ag_wait(h, s1, 3)
        if s1 == 0:
            ag(h, 0, 3, 2, 3, ring(h, 1, d))

    def stage_two(h, s1, s2):
        ag_wait(h, s1, s2)
        if s2 == 0:
            ag(h, s1, 0, s1, 2, ring(h, 2, d))

    from_holder = lax.rem(z - y + 4, 4)

    def rho_out():
        @pl.when(off_diag)
        def _():
            remote(
                rho_own, rho_in.at[from_holder], rho_send, rho_recv.at[from_holder], holder, keep=False
            ).start()

    strips = (2 * k, 2 - 2 * k, 1)

    def block_place(strip, t):
        column = lax.rem(row + strip - 1 + 32, 32)
        line = lax.rem(row + t - 1 + 32, 32)
        return column, line

    def v_copy(strip, t, which=0):
        column, line = block_place(strip, t)
        return remote(
            v_out.at[strip, t], v_in.at[2 - strip, t], v_send.at[which], v_recv.at[2 - strip, t],
            (column, line // 8), keep=False,
        )

    def on_holder(call):
        return lambda *args: pl.when(diag)(functools.partial(call, *args))

    @on_holder
    def window_points():
        for o in (1, 2, 3):
            arrived(rho_in.at[o], rho_recv.at[o])
        for slot in range(4):
            b = batch_of(slot)
            rho = rho_own[b] + rho_in[1, b] + rho_in[2, b] + rho_in[3, b]
            pot = packs[slot, 1:2, :] * (-slater_coef * jnp.exp(jnp.log(rho + 1.0) * (1.0 / 3.0)))
            pots[:, slot * 512 : slot * 512 + 512] = pot

    def scale_rows(strip):
        rows = pl.ds(pl.multiple_of(strip * 256, 256), 256)
        scaled[rows, :] = (spread[rows, :].astype(f32) * pots[...]).astype(bf16)
        return scaled[rows, :]

    @on_holder
    def window_strip(order):
        strip = strips[order]
        columns = scale_rows(strip)
        halves = [
            lax.dot_general(spread[i * 384 : i * 384 + 384], columns, NT, preferred_element_type=f32)
            for i in range(2)
        ]
        side = jnp.concatenate(halves, axis=0)
        for t in range(3):
            v_out[strip, t] = side[t * 256 : t * 256 + 256].astype(bf16)
        for t in (strip, 1, 2 - strip):
            v_copy(strip, t).start()
        crossing[order] = side[256:512]
        if order == 0:
            _, line = block_place(1, strip)

            @pl.when(line // 8 != z)
            def _():
                v_out[1, strip] = crossing[0].T.astype(bf16)
                v_copy(1, strip, 1 + strip // 2).start()

    @on_holder
    def window_centre():
        centre = lax.dot_general(spread[256:512], scale_rows(1), NT, preferred_element_type=f32)
        for order, strip in ((2, 1), (0, strips[0]), (1, strips[1])):
            total = centre if order == 2 else crossing[order].T
            _, line = block_place(1, strip)
            rows = pl.ds(pl.multiple_of(lax.rem(line, 8) * 256, 256), 256)
            if order == 0:

                @pl.when(line // 8 == z)
                def _():
                    pot_ref[rows, :] += total

            else:
                pot_ref[rows, :] += total

    late_panel = lax.rem(2 * z - y + 6, 4)
    late_own = lax.rem(z + 2, 4)
    first_early = lax.rem(late_panel + 1 + (late_own == lax.rem(late_panel + 1, 4)).astype(jnp.int32), 4)
    second_early = lax.rem(late_panel + 3 - (late_own == lax.rem(late_panel + 3, 4)).astype(jnp.int32), 4)

    def add_slices(indices, last, rows_of=lambda b: slices[b]):
        def quad_step(quad, carry):
            for i in range(2):
                rows = pl.ds(pl.multiple_of((2 * quad + i) * 512, 512), 512)
                total = sum(
                    lax.dot_general(
                        panel[pl.ds(4 * quad + 2 * i, 2), b].reshape(512, 512), rows_of(b), NT,
                        preferred_element_type=f32,
                    )
                    for b in indices
                )
                if last:
                    dens_ref[rows, :] = (2.0 * (dens_sum[rows, :] + total)).astype(bf16)
                else:
                    dens_sum[rows, :] = total
            return carry

        lax.fori_loop(0, 2, quad_step, 0)

    def density_early():
        pltpu.make_async_copy(c_ref, slices.at[z], load_sem.at[0]).wait()
        arrived(panel.at[0:3], mate_recv.at[0])

        @pl.when(diag)
        def _():
            add_slices([lax.rem(z + o, 4) for o in (0, 1, 3)], False, own_rows)

        @pl.when(off_diag)
        def _():
            z_wait(1)
            add_slices([first_early, second_early], False)

    def own_rows(b):
        return panel[x * 2 + k, b]

    def density_late():
        arrived(panel.at[0], mate_recv.at[1])

        @pl.when(diag)
        def _():
            add_slices([late_own], True, own_rows)

        @pl.when(off_diag)
        def _():
            z_wait(2)
            add_slices([late_panel, late_own], True)

    def left(ref, send_sem):
        pltpu.make_async_remote_copy(
            src_ref=ref, dst_ref=ref, send_sem=send_sem, recv_sem=mate_recv.at[0],
            device_id=mate, device_id_type=MESH,
        ).wait_send()

    def all_left():
        for ref, sem in (
            (panel.at[0:5, 0:3, part(0)], ag_send.at[0]), (panel.at[0:5, 0:3, part(1)], ag_send.at[1]),
            (panel.at[0:4], mate_send),
            (slices.at[0], z_send), (phis, phi_send), (packs.at[0:3], pack_send), (window, win_send),
        ):
            left(ref, sem)
        pl.when(lax.rem(z - d + 4, 4) != y)(lambda: left(slices.at[0], z_behind))
        pl.when(lax.rem(z + d + 4, 4) != y)(lambda: left(slices.at[0], z_ahead))

    steps = [
        (window_first, False), (phi_first, 0), (phi_first, 1), (phi_first, 2),
        (turn_wait, 0), (ag_first, 0), (phi_first, 3),
        (turn_wait, 1), (ag_first, 1), (ag_second, 0, 3), (ag_second, 1, 3),
        (to_mate, 0, 3, 3), (to_mate, 1, 3, 3), (pack_relay,), (select, 0), (select, 1),
        (stage_one, 0, 0), (window_first, True), (phi_relay, 0), (phi_relay, 1),
        (stage_one, 1, 0), (ag_second, 0, 0), (ag_second, 1, 0),
        (stage_one, 0, 1), (ag_second, 0, 1), (stage_one, 1, 1), (ag_second, 1, 1), (phi_relay, 2), (select, 2),
        (stage_two, 1, 3, 0), (stage_two, 0, 3, 0), (phi_relay, 3), (spread_batch, 0),
        (stage_one, 0, 2), (ag_second, 0, 2), (turn_window, 0), (turn_window, 2), (partial_rho, 3),
        (stage_one, 1, 2), (ag_second, 1, 2), (partial_rho, 0), (spread_arrived, 1), (z_first, 0), (partial_rho, 1),
        (stage_two, 1, 0, 0), (stage_two, 0, 0, 0), (stage_two, 1, 1, 0), (stage_two, 0, 1, 0),
        (spread_arrived, 2), (partial_rho, 2), (rho_out,), (z_first, 1), (z_relay, 0),
        (stage_two, 1, 2, 0), (stage_two, 0, 2, 0),
        (stage_two, 0, 3, 1), (stage_two, 1, 3, 1), (stage_two, 0, 0, 1), (stage_two, 1, 0, 1),
        (stage_two, 0, 3, 2), (stage_two, 1, 3, 2), (stage_two, 0, 1, 1), (stage_two, 1, 1, 1),
        (window_points,), (window_strip, 0), (z_relay, 1),
        (stage_two, 0, 2, 1), (stage_two, 1, 2, 1), (stage_two, 0, 0, 2), (stage_two, 1, 0, 2),
        (window_strip, 1),
        (stage_two, 1, 1, 2), (stage_two, 0, 1, 2), (stage_two, 0, 2, 2), (stage_two, 1, 2, 2),
        (density_early,), (window_centre,), (density_late,), (all_left,),
    ]
    for call, *args in steps:
        call(*args)

    for s in (1, 2 - 2 * k, 2 * k):
        for t in range(3):
            source = lax.rem(row + s - 1 + 32, 32)
            line = lax.rem(source + t - 1 + 32, 32)
            coming = line // 8 == z
            if isinstance(s, int):
                coming = jnp.logical_and(coming, source // 8 != z)

            @pl.when(coming)
            def _():
                arrived(v_in.at[s, t], v_recv.at[s, t])
                pot_ref[pl.ds(pl.multiple_of(lax.rem(line, 8) * 256, 256), 256), :] += v_in[s, t].astype(f32)

    @pl.when(off_diag)
    def _():
        left(own_piece, turn_send)
        left(rho_own, rho_send)

    @pl.when(diag)
    def _():
        left(v_out.at[0:2], v_send.at[0])
        for t in (0, 2):
            _, line = block_place(1, t)

            @pl.when(line // 8 != z)
            def _():
                left(v_out.at[1, t], v_send.at[1 + t // 2])


def store_results(density, potential, density_out, potential_out, sems):
    copies = []
    for source, target, pieces in ((potential, potential_out, 8), (density, density_out, 4)):
        for i in range(pieces):
            rows = pl.ds(i * (2048 // pieces), 2048 // pieces)
            copies.append(pltpu.make_async_copy(source.at[rows], target.at[rows], sems.at[len(copies)]))
    for copy in copies:
        copy.start()
    for copy in copies:
        copy.wait()


def on_device(coeffs, basis_values, point_weights, point_counts, func_lists):
    dma = pltpu.SemaphoreType.DMA
    density, potential = pl.pallas_call(
        kernel,
        out_shape=(
            pltpu.VMEM((2048, 256), bf16),
            pltpu.VMEM((2048, 256), f32),
        ),
        in_specs=[pl.BlockSpec(memory_space=pltpu.SMEM)] + [pl.BlockSpec(memory_space=pltpu.HBM)] * 4,
        out_specs=(pl.BlockSpec(memory_space=pltpu.VMEM),) * 2,
        scratch_shapes=[
            pltpu.VMEM((256, 512), bf16),
            pltpu.VMEM((512, 512), bf16),
            pltpu.VMEM((1, 512), jnp.int32),
            pltpu.VMEM((1, 512), f32),
            pltpu.VMEM((8, 4, 256, 512), bf16),
            pltpu.VMEM((4, 256, 512), bf16),
            pltpu.VMEM((2, 256, 512), bf16),
            pltpu.VMEM((3, 512, 512), bf16),
            pltpu.VMEM((4, 8, 512), f32),
            pltpu.VMEM((512, 768), bf16),
            pltpu.VMEM((4, 768, 512), bf16),
            pltpu.VMEM((768, 2048), bf16),
            pltpu.VMEM((768, 2048), bf16),
            pltpu.VMEM((4, 1, 512), f32),
            pltpu.VMEM((4, 4, 1, 512), f32),
            pltpu.VMEM((2, 256, 256), f32),
            pltpu.VMEM((1, 2048), f32),
            pltpu.VMEM((2048, 256), f32),
            pltpu.VMEM((3, 3, 256, 256), bf16),
            pltpu.VMEM((3, 3, 256, 256), bf16),
            dma((2,)), dma((2, 4, 4)), dma, dma((2,)),
            dma, dma, dma, dma((3, 2)), dma, dma((4,)), dma((2,)), dma, dma((3,)),
            dma, dma, dma((2,)), dma, dma((4,)), dma((3,)), dma((3, 3)), dma, dma((4,)),
        ],
        compiler_params=pltpu.CompilerParams(
            collective_id=0, has_side_effects=True, vmem_limit_bytes=36 * 1024 * 1024
        ),
    )(
        point_counts,
        *(
            pltpu.with_memory_space_constraint(array, pltpu.HBM)
            for array in (coeffs, basis_values.reshape(512, 512), func_lists, point_weights)
        ),
    )
    density, potential = (pltpu.with_memory_space_constraint(array, pltpu.VMEM) for array in (density, potential))
    return pl.pallas_call(
        store_results,
        out_shape=(
            jax.ShapeDtypeStruct((2048, 256), bf16),
            jax.ShapeDtypeStruct((2048, 256), f32),
        ),
        in_specs=[pl.BlockSpec(memory_space=pltpu.VMEM)] * 2,
        out_specs=(pl.BlockSpec(memory_space=pltpu.HBM),) * 2,
        scratch_shapes=[dma((12,))],
        compiler_params=pltpu.CompilerParams(vmem_limit_bytes=2 * 1024 * 1024),
    )(density, potential)


def solution(mesh):
    in_specs = (
        P("row", "col"),
        P(("row", "col"), None, None),
        P(("row", "col"), None),
        P(("row", "col")),
        P(("row", "col"), None),
    )
    out_specs = (P("col", "row"), P("col", "row"))
    return jax.shard_map(
        on_device, mesh=mesh, in_specs=in_specs, out_specs=out_specs, check_vma=False
    )
```

```python
import functools
import jax
import jax.numpy as jnp
from jax import lax
from jax.experimental import pallas as pl
from jax.experimental.pallas import tpu as pltpu
from jax.sharding import PartitionSpec as P

slater_coef = 0.9847450218426965
MESH = pl.DeviceIdType.MESH
f32 = jnp.float32
bf16 = jnp.bfloat16

OFFSET = (-1, 1, 2, 0)
ROWS = ((0, 112), (112, 144))
NT = (((1,), (1,)), ((), ()))


def kernel(
    count_ref, c_hbm, phi_hbm, list_hbm, weight_hbm, dens_ref, pot_ref,
    c_ref, phi_ref, list_ref, weight_ref,
    panel, slices, window, phis, packs, window_t, selectors, spread, scaled, rho_own, rho_in, crossing, pots, dens_sum, v_out, v_in,
    ag_send, ag_recv, mate_send, mate_recv, z_send, z_behind, z_ahead, z_recv, phi_send, phi_recv, phi_rest, pack_send, pack_recv,
    turn_send, win_send, win_recv, rho_send, rho_recv, v_send, v_recv, local_sem, load_sem,
):
    row = lax.axis_index("row")
    z = lax.axis_index("col")
    k = lax.rem(row, 2)
    x = lax.rem(row // 2, 4)
    y = row // 8
    d = 1 - 2 * k
    diag = y == z
    off_diag = y != z

    def place(dx=0, dy=0, dz=0, core=None):
        xx = lax.rem(x + dx + 8, 4)
        yy = lax.rem(y + dy + 8, 4)
        core = k if core is None else core
        return ((yy * 4 + xx) * 2 + core, lax.rem(z + dz + 8, 4))

    def shifted(dr, dz):
        return (lax.rem(row + dr + 32, 32), lax.rem(z + dz + 4, 4))

    mate = place(core=1 - k)
    turn_to = ((lax.rem(2 * y - z + 8, 4) * 4 + x) * 2 + k, y)
    turn_from = ((z * 4 + x) * 2 + k, lax.rem(2 * z - y + 8, 4))
    holder = (row, y)

    loads = [
        pltpu.make_async_copy(source, target, load_sem.at[i])
        for i, (source, target) in enumerate(
            ((list_hbm, list_ref), (weight_hbm, weight_ref), (phi_hbm, phi_ref), (c_hbm, c_ref))
        )
    ]
    for load in loads:
        load.start()
    barrier = pltpu.get_barrier_semaphore()
    friends = [mate, place(dx=1), place(dx=-1), place(dy=1), place(dy=-1), place(dz=2)]
    friends += [shifted(dr, dz) for dr in (-1, 0, 1) for dz in (-1, 0, 1) if dr or dz]
    for friend in friends:
        pl.semaphore_signal(barrier, inc=1, device_id=friend, device_id_type=MESH)

    @pl.when(off_diag)
    def _():
        for friend in (turn_to, turn_from):
            pl.semaphore_signal(barrier, inc=1, device_id=friend, device_id_type=MESH)

    def remote(src, dst, send_sem, recv_sem, device, keep=True):
        copy = pltpu.make_async_remote_copy(
            src_ref=src, dst_ref=dst, send_sem=send_sem, recv_sem=recv_sem,
            device_id=device, device_id_type=MESH,
        )
        if keep:
            copy.start()
        return copy

    def arrived(dst, recv_sem):
        pltpu.make_async_remote_copy(
            src_ref=dst, dst_ref=dst, send_sem=mate_send, recv_sem=recv_sem,
            device_id=mate, device_id_type=MESH,
        ).wait_recv()

    def part(h):
        return pl.ds(ROWS[h][0], ROWS[h][1])

    def piece(h, s1, s2, core=None):
        core_now, way = (k, d) if core is None else (1 - k, -d)
        first, second = (x, y) if h == 0 else (y, x)
        o1 = lax.rem(first + OFFSET[s1] * way + 8, 4)
        o2 = lax.rem(second + OFFSET[s2] * way + 8, 4)
        sx, sy = (o1, o2) if h == 0 else (o2, o1)
        return panel.at[sx * 2 + core_now, lax.rem(2 * z - sy + 8, 4), part(h)]

    def ring(h, stage, step):
        along_x = (h == 0) == (stage == 1)
        return place(dx=step) if along_x else place(dy=step)

    def ag(h, s1, s2, to1, to2, device):
        ref = piece(h, s1, s2)
        remote(ref, ref, ag_send.at[h], ag_recv.at[h, to1, to2], device)

    def ag_first(h):
        ag(h, 3, 3, 0, 3, ring(h, 1, d))
        ag(h, 3, 3, 1, 3, ring(h, 1, -d))

    def ag_second(h, s1):
        ag(h, s1, 3, s1, 0, ring(h, 2, d))
        ag(h, s1, 3, s1, 1, ring(h, 2, -d))

    def to_mate(h, s1, s2):
        ref = piece(h, s1, s2)
        late = (s2 if h == 0 else s1) == 2
        remote(ref, ref, mate_send, mate_recv.at[int(late)], mate)

    def ag_wait(h, s1, s2):
        arrived(piece(h, s1, s2), ag_recv.at[h, s1, s2])
        to_mate(h, s1, s2)

    own_piece = panel.at[x * 2 + k, z]
    pack_ref = packs.at[3]

    def phi_part(chunk):
        return pl.ds(chunk * 128, 128)

    def phi_first(chunk):
        for slot, way in ((0, d), (1, -d)):
            remote(
                phi_ref.at[phi_part(chunk)], phis.at[slot, phi_part(chunk)],
                phi_send, phi_recv.at[chunk] if slot == 0 else phi_rest.at[slot - 1], place(dz=way),
            )

    def phi_relay(chunk):
        ref = phis.at[0, phi_part(chunk)]
        arrived(ref, phi_recv.at[chunk])
        remote(ref, phis.at[2, phi_part(chunk)], phi_send, phi_rest.at[1], place(dz=d))

    def pack_first():
        remote(pack_ref, packs.at[0], pack_send, pack_recv.at[0], place(dz=d))
        remote(pack_ref, packs.at[1], pack_send, pack_recv.at[1], place(dz=-d))

    def pack_relay():
        arrived(packs.at[0], pack_recv.at[0])
        remote(packs.at[0], packs.at[2], pack_send, pack_recv.at[2], place(dz=d))
        arrived(packs.at[1], pack_recv.at[1])

    def z_part(half):
        return pl.ds(half * 128, 128)

    def z_first(half):
        remote(c_ref.at[z_part(half)], slices.at[z, z_part(half)], z_send, z_recv.at[0, half], place(dz=d))

        @pl.when(lax.rem(z - d + 4, 4) != y)
        def _():
            remote(
                c_ref.at[z_part(half)], slices.at[z, z_part(half)], z_behind, z_recv.at[1, half], place(dz=-d)
            )

    def z_relay(half):
        ref = slices.at[batch_of(0), z_part(half)]
        arrived(ref, z_recv.at[0, half])

        @pl.when(lax.rem(z + d + 4, 4) != y)
        def _():
            remote(ref, ref, z_ahead, z_recv.at[2, half], place(dz=d))

    def z_wait(slot):
        for half in range(2):
            arrived(slices.at[batch_of(slot), z_part(half)], z_recv.at[slot, half])

    def pack_own():
        window_start = lax.rem(row + 31, 32) * 256
        index = list_ref[...] - window_start
        packs[3, 0:1, :] = jnp.where(index < 0, index + 8192, index).astype(f32)
        point = lax.broadcasted_iota(jnp.int32, (1, 512), 1)
        packs[3, 1:2, :] = jnp.where(point < count_ref[0], weight_ref[...], 0.0)

    def zero_fill():
        pot_ref[...] = jnp.zeros_like(pot_ref)

    def select(slot):
        if slot == 2:
            arrived(packs.at[2], pack_recv.at[2])
        index = packs[slot, 0:1, :]
        slots = lax.broadcasted_iota(jnp.int32, (768, 512), 0).astype(f32)
        selectors[slot] = jnp.where(slots == index, 1.0, 0.0).astype(bf16)

    def spread_batch(slot):
        ref = phi_ref if slot == 3 else phis.at[slot]
        spread[:, slot * 512 : slot * 512 + 512] = lax.dot_general(
            selectors[slot], ref[...], NT, preferred_element_type=f32
        ).astype(bf16)

    def batch_of(slot):
        return lax.rem(z + OFFSET[slot] * d + 8, 4)

    def partial_rho(slot):
        mixed = jnp.dot(
            window_t[...], spread[:, slot * 512 : slot * 512 + 512], preferred_element_type=f32
        )
        rho_own[batch_of(slot)] = 2.0 * jnp.sum(mixed * mixed, axis=0, keepdims=True)

    def turn_window(side):
        if side == 1:
            window_t[:, 256:512] = c_ref[...].T
        else:
            index = side // 2
            arrived(window.at[index], win_recv.at[index])
            window_t[:, side * 256 : side * 256 + 256] = window[index].T

    def spread_arrived(slot):
        arrived(phis.at[slot], phi_rest.at[slot - 1])
        spread_batch(slot)

    zero_fill()
    loads[0].wait()
    loads[1].wait()
    pack_own()
    select(3)
    loads[2].wait()
    spread_batch(3)
    loads[3].wait()
    turn_window(1)
    pl.semaphore_wait(barrier, len(friends) + 2 * off_diag.astype(jnp.int32))

    pltpu.make_async_copy(c_ref, slices.at[z], load_sem.at[0]).start()

    @pl.when(off_diag)
    def _():
        for h in range(2):
            remote(
                c_ref.at[part(h)], own_piece.at[part(h)], turn_send, ag_recv.at[h, 3, 3], turn_to, keep=False
            ).start()

    @pl.when(diag)
    def _():
        pltpu.make_async_copy(c_ref, own_piece, local_sem).start()

    pack_first()

    def window_first(far):
        for side, dr, edge in ((0, 1, 7), (1, -1, 0)):
            is_far = lax.rem(row, 8) == edge

            @pl.when(is_far if far else jnp.logical_not(is_far))
            def _():
                remote(c_ref, window.at[side], win_send, win_recv.at[side], shifted(dr, 0))

    def turn_wait(h):
        @pl.when(off_diag)
        def _():
            arrived(piece(h, 3, 3), ag_recv.at[h, 3, 3])

        if h == 0:

            @pl.when(diag)
            def _():
                pltpu.make_async_copy(c_ref, own_piece, local_sem).wait()

    def stage_one(h, s1):
        ag_wait(h, s1, 3)
        if s1 == 0:
            ag(h, 0, 3, 2, 3, ring(h, 1, d))

    def stage_two(h, s1, s2):
        ag_wait(h, s1, s2)
        if s2 == 0:
            ag(h, s1, 0, s1, 2, ring(h, 2, d))

    from_holder = lax.rem(z - y + 4, 4)

    def rho_out():
        @pl.when(off_diag)
        def _():
            remote(
                rho_own, rho_in.at[from_holder], rho_send, rho_recv.at[from_holder], holder, keep=False
            ).start()

    strips = (2 * k, 2 - 2 * k, 1)

    def block_place(strip, t):
        column = lax.rem(row + strip - 1 + 32, 32)
        line = lax.rem(row + t - 1 + 32, 32)
        return column, line

    def v_copy(strip, t, which=0):
        column, line = block_place(strip, t)
        return remote(
            v_out.at[strip, t], v_in.at[2 - strip, t], v_send.at[which], v_recv.at[2 - strip, t],
            (column, line // 8), keep=False,
        )

    def on_holder(call):
        return lambda *args: pl.when(diag)(functools.partial(call, *args))

    @on_holder
    def window_points():
        for o in (1, 2, 3):
            arrived(rho_in.at[o], rho_recv.at[o])
        for slot in range(4):
            b = batch_of(slot)
            rho = rho_own[b] + rho_in[1, b] + rho_in[2, b] + rho_in[3, b]
            pot = packs[slot, 1:2, :] * (-slater_coef * jnp.exp(jnp.log(rho + 1.0) * (1.0 / 3.0)))
            pots[:, slot * 512 : slot * 512 + 512] = pot

    def scale_rows(strip):
        rows = pl.ds(pl.multiple_of(strip * 256, 256), 256)
        scaled[rows, :] = (spread[rows, :].astype(f32) * pots[...]).astype(bf16)
        return scaled[rows, :]

    @on_holder
    def window_strip(order):
        strip = strips[order]
        columns = scale_rows(strip)
        if order == 0:
            rows = spread[pl.ds(pl.multiple_of(strip * 256, 256), 256), :]
            corner = sum(
                lax.dot_general(rows[:, cut], columns[:, cut], NT, preferred_element_type=f32)
                for cut in (slice(0, 1024), slice(1024, 2048))
            )
            v_out[strip, strip] = corner.astype(bf16)
            v_copy(strip, strip).start()
            far = spread[pl.ds(pl.multiple_of((2 - strip) * 256, 256), 256), :]
            middle = lax.dot_general(spread[256:512], columns, NT, preferred_element_type=f32)
            last = lax.dot_general(far, columns, NT, preferred_element_type=f32)
            v_out[strip, 1] = middle.astype(bf16)
            v_copy(strip, 1).start()
            v_out[strip, 2 - strip] = last.astype(bf16)
            v_copy(strip, 2 - strip).start()
        else:
            halves = [
                lax.dot_general(spread[i * 384 : i * 384 + 384], columns, NT, preferred_element_type=f32)
                for i in range(2)
            ]
            side = jnp.concatenate(halves, axis=0)
            middle = side[256:512]
            for t in range(3):
                v_out[strip, t] = side[t * 256 : t * 256 + 256].astype(bf16)
            for t in range(3):
                v_copy(strip, t).start()
        crossing[order] = middle
        if order == 0:
            _, line = block_place(1, strip)

            @pl.when(line // 8 != z)
            def _():
                v_out[1, strip] = crossing[0].T.astype(bf16)
                v_copy(1, strip, 1 + strip // 2).start()

    @on_holder
    def window_centre():
        centre = lax.dot_general(spread[256:512], scale_rows(1), NT, preferred_element_type=f32)
        for order, strip in ((2, 1), (0, strips[0]), (1, strips[1])):
            total = centre if order == 2 else crossing[order].T
            _, line = block_place(1, strip)
            rows = pl.ds(pl.multiple_of(lax.rem(line, 8) * 256, 256), 256)
            if order == 0:

                @pl.when(line // 8 == z)
                def _():
                    pot_ref[rows, :] += total

            else:
                pot_ref[rows, :] += total

    late_panel = lax.rem(2 * z - y + 6, 4)
    late_own = lax.rem(z + 2, 4)
    first_early = lax.rem(late_panel + 1 + (late_own == lax.rem(late_panel + 1, 4)).astype(jnp.int32), 4)
    second_early = lax.rem(late_panel + 3 - (late_own == lax.rem(late_panel + 3, 4)).astype(jnp.int32), 4)

    def add_slices(indices, last, rows_of=lambda b: slices[b]):
        def quad_step(quad, carry):
            for i in range(2):
                rows = pl.ds(pl.multiple_of((2 * quad + i) * 512, 512), 512)
                total = sum(
                    lax.dot_general(
                        panel[pl.ds(4 * quad + 2 * i, 2), b].reshape(512, 512), rows_of(b), NT,
                        preferred_element_type=f32,
                    )
                    for b in indices
                )
                if last:
                    dens_ref[rows, :] = (2.0 * (dens_sum[rows, :] + total)).astype(bf16)
                else:
                    dens_sum[rows, :] = total
            return carry

        lax.fori_loop(0, 2, quad_step, 0)

    def density_early():
        pltpu.make_async_copy(c_ref, slices.at[z], load_sem.at[0]).wait()
        arrived(panel.at[0:3], mate_recv.at[0])

        @pl.when(diag)
        def _():
            add_slices([lax.rem(z + o, 4) for o in (0, 1, 3)], False, own_rows)

        @pl.when(off_diag)
        def _():
            z_wait(1)
            add_slices([first_early, second_early], False)

    def own_rows(b):
        return panel[x * 2 + k, b]

    def density_late():
        arrived(panel.at[0], mate_recv.at[1])

        @pl.when(diag)
        def _():
            add_slices([late_own], True, own_rows)

        @pl.when(off_diag)
        def _():
            z_wait(2)
            add_slices([late_panel, late_own], True)

    def left(ref, send_sem):
        pltpu.make_async_remote_copy(
            src_ref=ref, dst_ref=ref, send_sem=send_sem, recv_sem=mate_recv.at[0],
            device_id=mate, device_id_type=MESH,
        ).wait_send()

    def all_left():
        for ref, sem in (
            (panel.at[0:5, 0:3, part(0)], ag_send.at[0]), (panel.at[0:5, 0:3, part(1)], ag_send.at[1]),
            (panel.at[0:4], mate_send),
            (slices.at[0], z_send), (phis, phi_send), (packs.at[0:3], pack_send), (window, win_send),
        ):
            left(ref, sem)
        pl.when(lax.rem(z - d + 4, 4) != y)(lambda: left(slices.at[0], z_behind))
        pl.when(lax.rem(z + d + 4, 4) != y)(lambda: left(slices.at[0], z_ahead))

    steps = [
        (window_first, False), (phi_first, 0), (phi_first, 1), (phi_first, 2),
        (turn_wait, 0), (ag_first, 0), (phi_first, 3),
        (turn_wait, 1), (ag_first, 1), (ag_second, 0, 3), (ag_second, 1, 3),
        (to_mate, 0, 3, 3), (to_mate, 1, 3, 3), (pack_relay,), (select, 0), (select, 1),
        (stage_one, 0, 0), (window_first, True), (phi_relay, 0), (phi_relay, 1),
        (stage_one, 1, 0), (ag_second, 0, 0), (ag_second, 1, 0),
        (stage_one, 0, 1), (ag_second, 0, 1), (stage_one, 1, 1), (ag_second, 1, 1), (phi_relay, 2), (select, 2),
        (stage_two, 1, 3, 0), (stage_two, 0, 3, 0), (phi_relay, 3), (spread_batch, 0),
        (stage_one, 0, 2), (ag_second, 0, 2), (turn_window, 0), (turn_window, 2), (partial_rho, 3),
        (stage_one, 1, 2), (ag_second, 1, 2), (partial_rho, 0), (spread_arrived, 1), (z_first, 0), (partial_rho, 1),
        (stage_two, 1, 0, 0), (stage_two, 0, 0, 0), (stage_two, 1, 1, 0), (stage_two, 0, 1, 0),
        (spread_arrived, 2), (partial_rho, 2), (rho_out,), (z_first, 1), (z_relay, 0),
        (stage_two, 1, 2, 0), (stage_two, 0, 2, 0),
        (stage_two, 0, 3, 1), (stage_two, 1, 3, 1), (stage_two, 0, 0, 1), (stage_two, 1, 0, 1),
        (stage_two, 0, 3, 2), (stage_two, 1, 3, 2), (stage_two, 0, 1, 1), (stage_two, 1, 1, 1),
        (window_points,), (window_strip, 0), (z_relay, 1),
        (stage_two, 0, 2, 1), (stage_two, 1, 2, 1), (stage_two, 0, 0, 2), (stage_two, 1, 0, 2),
        (window_strip, 1),
        (stage_two, 1, 1, 2), (stage_two, 0, 1, 2), (stage_two, 0, 2, 2), (stage_two, 1, 2, 2),
        (density_early,), (window_centre,), (density_late,), (all_left,),
    ]
    for call, *args in steps:
        call(*args)

    for s in (1, 2 - 2 * k, 2 * k):
        for t in range(3):
            source = lax.rem(row + s - 1 + 32, 32)
            line = lax.rem(source + t - 1 + 32, 32)
            coming = line // 8 == z
            if isinstance(s, int):
                coming = jnp.logical_and(coming, source // 8 != z)

            @pl.when(coming)
            def _():
                arrived(v_in.at[s, t], v_recv.at[s, t])
                pot_ref[pl.ds(pl.multiple_of(lax.rem(line, 8) * 256, 256), 256), :] += v_in[s, t].astype(f32)

    @pl.when(off_diag)
    def _():
        left(own_piece, turn_send)
        left(rho_own, rho_send)

    @pl.when(diag)
    def _():
        left(v_out.at[0:2], v_send.at[0])
        for t in (0, 2):
            _, line = block_place(1, t)

            @pl.when(line // 8 != z)
            def _():
                left(v_out.at[1, t], v_send.at[1 + t // 2])


def store_results(density, potential, density_out, potential_out, sems):
    copies = []
    for source, target, pieces in ((potential, potential_out, 8), (density, density_out, 4)):
        for i in range(pieces):
            rows = pl.ds(i * (2048 // pieces), 2048 // pieces)
            copies.append(pltpu.make_async_copy(source.at[rows], target.at[rows], sems.at[len(copies)]))
    for copy in copies:
        copy.start()
    for copy in copies:
        copy.wait()


def on_device(coeffs, basis_values, point_weights, point_counts, func_lists):
    dma = pltpu.SemaphoreType.DMA
    density, potential = pl.pallas_call(
        kernel,
        out_shape=(
            pltpu.VMEM((2048, 256), bf16),
            pltpu.VMEM((2048, 256), f32),
        ),
        in_specs=[pl.BlockSpec(memory_space=pltpu.SMEM)] + [pl.BlockSpec(memory_space=pltpu.HBM)] * 4,
        out_specs=(pl.BlockSpec(memory_space=pltpu.VMEM),) * 2,
        scratch_shapes=[
            pltpu.VMEM((256, 512), bf16),
            pltpu.VMEM((512, 512), bf16),
            pltpu.VMEM((1, 512), jnp.int32),
            pltpu.VMEM((1, 512), f32),
            pltpu.VMEM((8, 4, 256, 512), bf16),
            pltpu.VMEM((4, 256, 512), bf16),
            pltpu.VMEM((2, 256, 512), bf16),
            pltpu.VMEM((3, 512, 512), bf16),
            pltpu.VMEM((4, 8, 512), f32),
            pltpu.VMEM((512, 768), bf16),
            pltpu.VMEM((4, 768, 512), bf16),
            pltpu.VMEM((768, 2048), bf16),
            pltpu.VMEM((768, 2048), bf16),
            pltpu.VMEM((4, 1, 512), f32),
            pltpu.VMEM((4, 4, 1, 512), f32),
            pltpu.VMEM((2, 256, 256), f32),
            pltpu.VMEM((1, 2048), f32),
            pltpu.VMEM((2048, 256), f32),
            pltpu.VMEM((3, 3, 256, 256), bf16),
            pltpu.VMEM((3, 3, 256, 256), bf16),
            dma((2,)), dma((2, 4, 4)), dma, dma((2,)),
            dma, dma, dma, dma((3, 2)), dma, dma((4,)), dma((2,)), dma, dma((3,)),
            dma, dma, dma((2,)), dma, dma((4,)), dma((3,)), dma((3, 3)), dma, dma((4,)),
        ],
        compiler_params=pltpu.CompilerParams(
            collective_id=0, has_side_effects=True, vmem_limit_bytes=36 * 1024 * 1024
        ),
    )(
        point_counts,
        *(
            pltpu.with_memory_space_constraint(array, pltpu.HBM)
            for array in (coeffs, basis_values.reshape(512, 512), func_lists, point_weights)
        ),
    )
    density, potential = (pltpu.with_memory_space_constraint(array, pltpu.VMEM) for array in (density, potential))
    return pl.pallas_call(
        store_results,
        out_shape=(
            jax.ShapeDtypeStruct((2048, 256), bf16),
            jax.ShapeDtypeStruct((2048, 256), f32),
        ),
        in_specs=[pl.BlockSpec(memory_space=pltpu.VMEM)] * 2,
        out_specs=(pl.BlockSpec(memory_space=pltpu.HBM),) * 2,
        scratch_shapes=[dma((12,))],
        compiler_params=pltpu.CompilerParams(vmem_limit_bytes=2 * 1024 * 1024),
    )(density, potential)


def solution(mesh):
    in_specs = (
        P("row", "col"),
        P(("row", "col"), None, None),
        P(("row", "col"), None),
        P(("row", "col")),
        P(("row", "col"), None),
    )
    out_specs = (P("col", "row"), P("col", "row"))
    return jax.shard_map(
        on_device, mesh=mesh, in_specs=in_specs, out_specs=out_specs, check_vma=False
    )
```
